128 devices in a mesh: chip: 64 (over x, y, z), cores: 2 (over core).
Axes of the slice: x: 4, y: 4, z: 4, core: 2. Of those that a mesh axis runs over, the one named last changes fastest.
Arguments:
- patch_field: float32 [2048, 6, 128, 128], P(('chip', 'cores')), may hold values from -6 to 6
- patch_tables: float32 [2048, 6, 128, 128], P(('chip', 'cores')), may hold values from -0.5 to 0.5
- coupling: float32 [2048, 5, 6, 6], P(('chip', 'cores')), may hold values from -1 to 1
- side_device: int32 [16384, 1], replicated, may hold values from 0 to 127; in each aligned block of 128 rows (0 to 127, 128 to 255, ...) at most 2 rows name the same one
- side_detail: int32 [16384, 4], replicated, may hold values from 0 to 96, as said below
- penalty: float32 [8192, 2, 128], P(('chip', 'cores')), may hold values from 0.1 to 1
- angles: float32 [8192, 3], P(('chip', 'cores')), may hold values from -3.140625 to 3.140625
Outputs:
- response: float32 [2048, 6, 128, 128], P(('chip', 'cores'))
The draws below stay inside these ranges and needn't reach their ends.
Inputs may be any that keep to these rules, and one draw needn't show every extreme that they name: `side_device`: in each aligned block of 128 rows (the sides of the interfaces whose quadrature one device owns) no device is named by more than 2 rows, and some device is named by exactly 2 rows. Each owner has exactly 128 sides. `side_detail`: column 0 is below 16, column 1 below 4, column 2 below 32, column 3 from 64 to 96.
All inputs are finite; a program needn't handle non-finite values.
Results may differ from the reference program's by a relative error of at most 0.0003.
Values sent between devices are 32-bit elements; how exact they have to be, the bound alone decides.
A program may use at most 192 MiB of HBM per device.

```python
import math
import jax
import jax.numpy as jnp
import numpy as np
from jax import lax

NP = 128
Q = 128
P_DEV = 16
IF_DEV = 64
NPATCH = 2048
IFACES = 8192
SIDES = 16384
CAP = 2
N_CHIP = 64
N_CORES = 2


def draw_side_detail(key, part):
    keys = jax.random.split(jax.random.fold_in(key, 17), 4)
    local = jax.random.randint(keys[0], (SIDES,), 0, P_DEV)
    edges = jax.random.randint(keys[1], (SIDES,), 0, 4)
    starts = jax.random.randint(keys[2], (SIDES,), 0, NP // 4)
    lengths = jax.random.randint(keys[3], (SIDES,), NP // 2, NP // 2 + NP // 4 + 1)
    return jnp.stack([local, edges, starts, lengths], axis=1).astype(jnp.int32)


def block_scale(rng, extent, cuts, smallest, top_value):
    gain = 1.0
    for axis_at, shards_of in cuts:
        steps = jax.random.uniform(jax.random.fold_in(jax.random.fold_in(rng, 6), axis_at), (shards_of,), jnp.float32, smallest / len(cuts), top_value / len(cuts))
        gain = gain * jnp.repeat(jnp.exp(steps), extent[axis_at] // shards_of).reshape((-1,) + (1,) * (len(extent) - 1 - axis_at))
    return gain


def assign_block(key, own, number, rows, count, top, reach, lean):
    sequence = jax.random.permutation(key, count)
    crowded, common = load_shares(count, rows * top, reach, lean, True), load_shares(count, rows * top, reach, lean, False)
    places = jnp.arange(count)

    def named(sizes, offset_by):
        used = int((sizes > 0).sum())
        fixed = max(1, used // 4)
        moved = fixed + (places - fixed + offset_by * (used - fixed)) % max(1, count - fixed)
        return jnp.zeros((count,), jnp.int32).at[sequence[jnp.where(places < fixed, places, moved)]].set(jnp.asarray(sizes, jnp.int32))

    sizes = jnp.where(number % 4 == 0, named(crowded, number // 4), named(common, number - number // 4 - 1))
    mixed = jax.random.permutation(jax.random.fold_in(own, 3), count)
    donor, sink = mixed[0:count // 2 * 2:2], mixed[1:count // 2 * 2:2]
    slack = jnp.minimum(sizes[donor] - 1, reach - sizes[sink]) // 2
    slack = jnp.where((donor == sequence[0]) | (sink == sequence[0]) | (sizes[sink] == 0), 0, jnp.maximum(slack, 0))
    moved = jax.random.randint(jax.random.fold_in(own, 4), (count // 2,), 0, 1 << 20) % (slack + 1)
    sizes = sizes.at[donor].add(-moved).at[sink].add(moved)
    members = jnp.searchsorted(jnp.cumsum(sizes), jnp.arange(rows * top), side="right").astype(jnp.int32)
    table = members.reshape(top, rows).T
    table = table[jax.random.permutation(jax.random.fold_in(own, 1), rows)]
    offset_by = jax.random.randint(jax.random.fold_in(own, 2), (rows, 1), 0, top)
    return jnp.take_along_axis(table, (jnp.arange(top)[None, :] + offset_by) % top, axis=1)


def load_shares(amount, total, most, slope, full):
    portions = [(1 << 20) // math.isqrt(rank ** slope) + 1 for rank in range(1, amount + 1)]
    largest = most if full else min(most, max(-(-total // amount), total * portions[0] // sum(portions)))
    least = 1 if total - largest >= amount - 1 else 0
    holding, spare = [largest] + [least] * (amount - 1), total - largest - least * (amount - 1)
    while spare > 0:
        movable = [i for i in range(1, amount) if holding[i] < largest] or [i for i in range(1, amount) if holding[i] < most]
        mass, remaining = sum([portions[i] for i in movable]), spare
        for i in movable:
            extra = min(most - holding[i], max(1, remaining * portions[i] // mass), spare)
            holding[i] = holding[i] + extra
            spare = spare - extra
    return np.array(holding)


def normal_values(rng, extent, spread, reach, cuts=(), kind=jnp.bfloat16):
    level = block_scale(rng, extent, cuts, -0.22, 0.18) if cuts else 1.0
    drawn = jax.random.normal(rng, extent, jnp.float32) * spread * level
    return jnp.minimum(jnp.maximum(drawn, -reach), reach).astype(kind)


def setup_inputs(seed: int = 0) -> dict:
    splits = jax.random.split(jax.random.key(seed), 8)
    patch_field = normal_values(splits[0], (NPATCH, 6, NP, NP), 1.0, 6.0, ((0, 128),), jnp.float32)
    patch_tables = normal_values(splits[1], (NPATCH, 6, NP, NP), NP ** -0.5, 0.5, ((0, 128),), jnp.float32)
    coupling = normal_values(splits[2], (NPATCH, 5, 6, 6), 30 ** -0.5, 1.0, ((0, 128),), jnp.float32)
    side_device_keys = jax.random.split(jax.random.fold_in(splits[3], 1), SIDES // (2 * IF_DEV))
    side_device_turns = jax.random.permutation(jax.random.fold_in(splits[3], 3), SIDES // (2 * IF_DEV))
    side_device = jax.vmap(lambda own, number: assign_block(jax.random.fold_in(splits[3], 2), own, number, 2 * IF_DEV, N_CHIP * N_CORES, 1, CAP, 2))(side_device_keys, side_device_turns).reshape((SIDES, 1))
    side_detail = draw_side_detail(jax.random.fold_in(splits[7], 71), 0)
    penalty = jnp.clip(jnp.exp(math.log(1.0) - 2.3025851 * jax.random.uniform(splits[5], (IFACES, 2, Q), jnp.float32) ** block_scale(splits[5], (IFACES, 2, Q), ((0, 128),), -0.2, 0.2)), 0.1, 1.0)
    angles = jnp.clip(jax.random.uniform(splits[6], (IFACES, 3), jnp.float32, -3.140625, 3.140625), -3.140625, 3.140625)
    return {"patch_field": patch_field, "patch_tables": patch_tables, "coupling": coupling, "side_device": side_device, "side_detail": side_detail, "penalty": penalty, "angles": angles}


HIGHEST = lax.Precision.HIGHEST


def interior_apply(field_block, table_block, coupling_block):
    def left_apply(matrix):
        return jnp.einsum('pij,pcjk->pcik', matrix, field_block, precision=HIGHEST)

    def right_apply(values, matrix):
        return jnp.einsum('pcik,plk->pcil', values, matrix, precision=HIGHEST)

    stiff_x = left_apply(table_block[:, 0])
    mass_x = left_apply(table_block[:, 1])
    slope_x = left_apply(table_block[:, 2])
    terms_all = jnp.stack([right_apply(stiff_x, table_block[:, 4]), right_apply(mass_x, table_block[:, 3]),
                           right_apply(slope_x, table_block[:, 5]), right_apply(mass_x, table_block[:, 4]),
                           right_apply(slope_x, table_block[:, 4])], axis=1)
    return jnp.einsum('ptcd,ptdij->pcij', coupling_block, terms_all, precision=HIGHEST)


def edge_strips(field_block):
    first = field_block[:, :, 0:2, :]
    second = field_block[:, :, ::-1, :][:, :, 0:2, :]
    third = jnp.swapaxes(field_block[:, :, :, 0:2], 2, 3)
    fourth = jnp.swapaxes(field_block[:, :, :, ::-1][:, :, :, 0:2], 2, 3)
    return jnp.stack([first, second, third, fourth], axis=1)


def add_edges(output, forces):
    count = output.shape[-1]
    output = output.at[:, :, 0:2, :].add(forces[:, 0])
    output = output.at[:, :, count - 2:count, :].add(forces[:, 1][:, :, ::-1, :])
    output = output.at[:, :, :, 0:2].add(jnp.swapaxes(forces[:, 2], 2, 3))
    output = output.at[:, :, :, count - 2:count].add(jnp.swapaxes(forces[:, 3], 2, 3)[:, :, :, ::-1])
    return output


def spline_weight(offset):
    magnitude = jnp.abs(offset)
    inner = 0.75 - magnitude * magnitude
    outer = 0.5 * jnp.square(jnp.maximum(1.5 - magnitude, 0.0))
    return jnp.where(magnitude < 0.5, inner, outer)


def extraction(starts, lengths, quad_count, point_count):
    quad_pos = jnp.arange(quad_count, dtype=jnp.int32).astype(jnp.float32) + 0.5
    points = jnp.arange(point_count, dtype=jnp.int32).astype(jnp.float32)
    param = starts.astype(jnp.float32)[:, None] + quad_pos[None, :] * lengths.astype(jnp.float32)[:, None] / quad_count
    return spline_weight(param[:, :, None] - points[None, None, :])


def edge_traces(basis, strip_data):
    combined = 1.5 * strip_data[:, :, 0, :] - 0.5 * strip_data[:, :, 1, :]
    return jnp.einsum('sqj,scj->scq', basis, combined, precision=HIGHEST)


def spread_back(basis, loads):
    summed = jnp.einsum('sqj,scq->scj', basis, loads, precision=HIGHEST)
    return jnp.stack([1.5 * summed, -0.5 * summed], axis=2)


def frame_maps(angle_data):
    cos_a, sin_a = jnp.cos(angle_data[:, 0]), jnp.sin(angle_data[:, 0])
    cos_b, sin_b = jnp.cos(angle_data[:, 1]), jnp.sin(angle_data[:, 1])
    cos_g, sin_g = jnp.cos(angle_data[:, 2]), jnp.sin(angle_data[:, 2])
    row_one = jnp.stack([cos_g * cos_b, cos_g * sin_b * sin_a - sin_g * cos_a, cos_g * sin_b * cos_a + sin_g * sin_a], axis=1)
    row_two = jnp.stack([sin_g * cos_b, sin_g * sin_b * sin_a + cos_g * cos_a, sin_g * sin_b * cos_a - cos_g * sin_a], axis=1)
    row_three = jnp.stack([-sin_b, cos_b * sin_a, cos_b * cos_a], axis=1)
    rotation = jnp.stack([row_one, row_two, row_three], axis=1)
    zeroes = jnp.zeros_like(rotation)
    upper = jnp.concatenate([rotation, zeroes], axis=2)
    lower = jnp.concatenate([zeroes, rotation], axis=2)
    return jnp.concatenate([upper, lower], axis=1)


def penalty_loads(trace_data, penalty_data, angle_data):
    owned = penalty_data.shape[0]
    paired = trace_data.reshape((owned, 2) + trace_data.shape[1:])
    frames = frame_maps(angle_data)
    jump_data = paired[:, 0] - jnp.einsum('icd,idq->icq', frames, paired[:, 1], precision=HIGHEST)
    weights = jnp.repeat(penalty_data, 3, axis=1)
    first_load = weights * jump_data
    second_load = -jnp.einsum('idc,idq->icq', frames, first_load, precision=HIGHEST)
    return jnp.stack([first_load, second_load], axis=1).reshape(trace_data.shape)


def reference(patch_field, patch_tables, coupling, side_device, side_detail, penalty, angles):
    blocks = NPATCH // P_DEV

    def shaped(array):
        return array.reshape((blocks, P_DEV) + array.shape[1:])

    def block_apply(parts_in):
        return interior_apply(parts_in[0], parts_in[1], parts_in[2])

    result = lax.map(block_apply, (shaped(patch_field), shaped(patch_tables), shaped(coupling))).reshape(patch_field.shape)
    strips_all = edge_strips(patch_field).reshape(NPATCH * 4, 6, 2, NP)
    owners = IFACES // IF_DEV

    def one_owner(parts_in):
        devices_in, detail_in, penalty_in, angle_in = parts_in
        strip_rows = ((devices_in * P_DEV + detail_in[:, 0]) * 4 + detail_in[:, 1]).astype(jnp.int32)
        gathered = strips_all[strip_rows]
        basis = extraction(detail_in[:, 2], detail_in[:, 3], Q, NP)
        loads = penalty_loads(edge_traces(basis, gathered), penalty_in, angle_in)
        return spread_back(basis, loads), strip_rows

    forces, strip_rows = lax.map(one_owner, (side_device.reshape(owners, 2 * IF_DEV),
                                             side_detail.reshape(owners, 2 * IF_DEV, 4),
                                             penalty.reshape(owners, IF_DEV, 2, Q),
                                             angles.reshape(owners, IF_DEV, 3)))
    edge_forces = jax.ops.segment_sum(forces.reshape(SIDES, 6, 2, NP), strip_rows.reshape(SIDES), num_segments=NPATCH * 4)
    return add_edges(result, edge_forces.reshape(NPATCH, 4, 6, 2, NP))
```

```python
import functools

import jax
import jax.numpy as jnp
from jax import lax
from jax.experimental import pallas as pl
from jax.experimental.pallas import tpu as pltpu
from jax.sharding import PartitionSpec as P

BF = jnp.bfloat16
F32 = jnp.float32
MESH = pl.DeviceIdType.MESH
CH = 16
TABLES = ((0, 0, None), (1, 3, (1, 1)), (2, 4, (2, 2)))


def split(x):
    high = x.astype(BF)
    return high, (x - high.astype(F32)).astype(BF)


def dot(a, b):
    return lax.dot_general(a, b, (((1,), (0,)), ((), ())), preferred_element_type=F32)


def dot_t(a, b):
    return lax.dot_general(a, b, (((1,), (1,)), ((), ())), preferred_element_type=F32)


def prep_field(field, ucat, c):
    h, l = split(field[c])
    cols = slice(c * 128, c * 128 + 128)
    ucat[0:128, cols] = h
    ucat[128:256, cols] = l
    ucat[256:384, cols] = h


def prep_left(tables, tcat, t):
    h, l = split(tables[t])
    rows = slice(t * 128, t * 128 + 128)
    tcat[rows, 0:128] = h
    tcat[rows, 128:256] = h
    tcat[rows, 256:384] = l


def prep_right(tables, rcat, s):
    h, l = split(tables[(4, 3, 5)[s]])
    cols = slice(s * 128, s * 128 + 128)
    rcat[0:128, cols] = h
    rcat[128:256, cols] = l


def prep_coupling(coup, cb, t):
    tile = coup[t]
    for d in range(6):
        cb[t * 6 + d] = jnp.broadcast_to(tile[:, d : d + 1], (6, 128))


def left_products(tcat, ucat, prod):
    prod[...] = dot(tcat[...], ucat[...])


def right_products(mixed, rcat, out):
    o = dot_t(mixed[:, 0:384], rcat[...])
    o2 = dot_t(mixed[:, 384:768], rcat[0:128, :])
    for c in range(6):
        q = slice(c * 128, c * 128 + 128)
        out[c] = (o[q, 0:128] + o[q, 128:256]) + o2[q]


def mix(prod, cb, mixed, r):
    def put(s, c, acc):
        h, l = split(acc)
        rows = slice(c * 128 + r, c * 128 + r + CH)
        mixed[rows, s * 128 : s * 128 + 128] = h
        mixed[rows, 384 + s * 128 : 384 + s * 128 + 128] = l

    def coef(t, c, d):
        return jnp.broadcast_to(cb[t * 6 + d, c : c + 1, :], (CH, 128))

    main = [None] * 6
    for t, term, other in TABLES:
        side = [None] * 6
        for d in range(6):
            x = prod[t * 128 + r : t * 128 + r + CH, d * 128 : d * 128 + 128]
            for c in range(6):
                v = x * coef(term, c, d)
                main[c] = v if main[c] is None else main[c] + v
                if other:
                    v = x * coef(other[0], c, d)
                    side[c] = v if side[c] is None else side[c] + v
        if other:
            for c in range(6):
                put(other[1], c, side[c])
    for c in range(6):
        put(0, c, main[c])


def spline(v):
    m = jnp.abs(v)
    far = jnp.maximum(1.5 - m, 0.0)
    return jnp.where(m < 0.5, 0.75 - m * m, 0.5 * far * far)


def iota(shape, axis):
    return lax.broadcasted_iota(jnp.int32, shape, axis)


def main_kernel(
    devs, inner, code, penalty, angles, field_hbm, tables_hbm, coup_hbm, part_hbm, force,
    uv, tv, cv, ov, u0, u1, t0, t1, r0, r1, p0, p1, w0, w1, b0, b1,
    comb, ccat, acat, picker, picker_t, taker, taker_t, wts, idx, sbuf, rbuf, bbuf, fbuf,
    in_sem, out_sem, send_sem, recv_sem, self_sem,
):
    n = uv.shape[0]
    me = lax.axis_index(("chip", "cores"))

    def where_is(p):
        return (p // inner, p % inner)

    barrier = pltpu.get_barrier_semaphore()

    def greet(i, carry):
        p = lax.rem(me + i, devs)
        pl.semaphore_signal(barrier, inc=1, device_id=where_is(p), device_id_type=MESH)
        return carry

    groups = 4
    per = n // groups
    loads_u = [
        pltpu.make_async_copy(
            field_hbm.at[pl.ds(g * per, per)], uv.at[pl.ds(g * per, per)], in_sem.at[g]
        )
        for g in range(groups)
    ]
    loads_t = [
        pltpu.make_async_copy(
            tables_hbm.at[pl.ds(g * per, per)], tv.at[pl.ds(g * per, per)], in_sem.at[groups + g]
        )
        for g in range(groups)
    ]
    load_c = pltpu.make_async_copy(coup_hbm, cv, in_sem.at[2 * groups])
    for copy in loads_u + loads_t + [load_c]:
        copy.start()
    lax.fori_loop(1, devs, greet, 0)

    full = code[...]
    lane = iota((128, 128), 1)
    sub = iota((128, 128), 0)
    lane_f = lane.astype(F32)
    sub_f = sub.astype(F32)
    eye = lane == sub
    hit = (full & 127) == me
    rid = (full >> 19).astype(F32)
    first = jnp.min(jnp.where(hit, lane_f, 1e6), axis=1, keepdims=True)
    last = jnp.max(jnp.where(hit, lane_f, -1.0), axis=1, keepdims=True)
    row0 = jnp.sum(jnp.where(lane_f == first, rid, 0.0), axis=1, keepdims=True)
    row1 = jnp.sum(jnp.where(lane_f == last, rid, 0.0), axis=1, keepdims=True)
    row0 = jnp.where(last >= 0.0, row0, -1.0)
    row1 = jnp.where(last > first, row1, -1.0)

    def to_row(col):
        return jnp.sum(jnp.where(eye, col, 0.0), axis=0, keepdims=True)

    def one_hot(mask):
        return jnp.where(mask, 1.0, 0.0).astype(BF)

    edge_lane = (lane & 63).astype(F32)
    edge_sub = iota((64, 128), 0).astype(F32)
    for k, row in enumerate((row0, row1)):
        picker[k * 128 : k * 128 + 128, :] = one_hot(row == edge_lane)
        flat = one_hot(to_row(row) == edge_sub)
        picker_t[:, k * 256 : k * 256 + 128] = flat
        picker_t[:, k * 256 + 128 : k * 256 + 256] = flat

    mine = code[pl.ds(me, 1), :]
    dev_row = (mine & 127).astype(F32)
    ln_row = ((mine >> 7) & 127).astype(F32)
    st_row = ((mine >> 14) & 31).astype(F32)
    order = jnp.where(sub < 64, 2 * sub, 2 * sub - 127)
    perm = lane == order

    def to_col(row):
        return jnp.sum(jnp.where(perm, row, 0.0), axis=1, keepdims=True)

    dev_col, ln, st = to_col(dev_row), to_col(ln_row), to_col(st_row)
    slot = jnp.sum(
        jnp.where((dev_row == dev_col) & (lane < order), 1.0, 0.0), axis=1, keepdims=True
    )
    dev_flat, slot_flat = to_row(dev_col), to_row(slot)
    for k in range(2):
        t = one_hot((lane_f == dev_col) & (slot == float(k)))
        taker[:, k * 256 : k * 256 + 128] = t
        taker[:, k * 256 + 128 : k * 256 + 256] = t
        t = one_hot((sub_f == dev_flat) & (slot_flat == float(k)))
        taker_t[k * 128 : k * 128 + 128, 0:128] = t
        taker_t[k * 128 : k * 128 + 128, 128:256] = t

    def strips(p, carry):
        for c in range(6):
            x = uv[p, c]
            y = jnp.transpose(pltpu.roll(x, 2, 1)[:, 0:8])
            comb[p, c : c + 1, :] = 1.5 * x[0:1] - 0.5 * x[1:2]
            comb[n + p, c : c + 1, :] = 1.5 * x[127:128] - 0.5 * x[126:127]
            comb[2 * n + p, c : c + 1, :] = 1.5 * y[2:3] - 0.5 * y[3:4]
            comb[3 * n + p, c : c + 1, :] = 1.5 * y[1:2] - 0.5 * y[0:1]
        return carry

    for g in range(groups):
        loads_u[g].wait()
        lax.fori_loop(g * per, (g + 1) * per, strips, 0)
    for c in range(6):
        h, l = split(comb[:, c, :])
        ccat[0:64, c * 128 : c * 128 + 128] = h
        ccat[64:128, c * 128 : c * 128 + 128] = l
    for k in range(2):
        slots = dot(picker[k * 128 : k * 128 + 128, :], ccat[...])
        for c in range(6):
            sbuf[:, k * 6 + c, :] = slots[:, c * 128 : c * 128 + 128]
    pl.semaphore_wait(barrier, devs - 1)

    def exchange(src, dst, which):
        def send(i, carry):
            p = lax.rem(me + 1 + lax.rem(i * 45, devs - 1), devs)
            pltpu.make_async_remote_copy(
                src_ref=src.at[p],
                dst_ref=dst.at[me],
                send_sem=send_sem.at[which],
                recv_sem=recv_sem.at[which],
                device_id=where_is(p),
                device_id_type=MESH,
            ).start()
            return carry

        lax.fori_loop(0, devs - 1, send, 0)
        pltpu.make_async_copy(src.at[me], dst.at[me], self_sem.at[which]).start()

    def settle(src, dst, which):
        others = pl.ds(0, devs - 1)
        pltpu.make_async_copy(src.at[others], dst.at[others], send_sem.at[which]).wait()
        pltpu.make_async_copy(src.at[others], dst.at[others], recv_sem.at[which]).wait()
        pltpu.make_async_copy(src.at[me], dst.at[me], self_sem.at[which]).wait()

    exchange(sbuf, rbuf, 0)

    unit = st * 256.0 + (2.0 * lane_f + 1.0) * ln
    near = jnp.floor((unit + 128.0) * (1.0 / 256.0))
    for tap in range(3):
        j = near + float(tap - 1)
        w = spline(unit * (1.0 / 256.0) - j)
        wts[tap] = jnp.where((j >= 0.0) & (j <= 127.0), w, 0.0)
        idx[tap] = jnp.clip(j, 0.0, 127.0).astype(jnp.int32)
    low = jnp.floor(((256.0 * (lane_f - st) - 384.0) / ln - 1.0) * 0.5) + 1.0
    for tap in range(6):
        q = low + float(tap)
        v = (st * 256.0 + (2.0 * q + 1.0) * ln) * (1.0 / 256.0) - lane_f
        wts[3 + tap] = jnp.where((q >= 0.0) & (q <= 127.0), spline(v), 0.0)
        idx[3 + tap] = jnp.clip(q, 0.0, 127.0).astype(jnp.int32)

    bufs = ((u0, t0, r0, p0, w0, b0), (u1, t1, r1, p1, w1, b1))
    load_c.wait()
    for copy in loads_t:
        copy.wait()

    def patch_out(p):
        return pltpu.make_async_copy(ov.at[p], part_hbm.at[p], out_sem)

    def stage(p, j):
        u, t, r, pr, w, b = bufs[j]
        un, tn, rn, prn, wn, bn = bufs[1 - j]
        before = jnp.maximum(p - 1, 0)
        after = jnp.minimum(p + 1, n - 1)
        later = jnp.minimum(p + 2, n - 1)
        seqs = (
            [lambda k=k: mix(pr, b, w, k * CH) for k in range(128 // CH)],
            [
                lambda: left_products(tn, un, prn),
                lambda: right_products(wn, rn, ov.at[before]),
            ],
            [lambda c=c: prep_field(uv.at[later], u, c) for c in range(6)]
            + [lambda k=k: prep_left(tv.at[later], t, k) for k in range(3)]
            + [lambda k=k: prep_right(tv.at[p], r, k) for k in range(3)],
            [lambda k=k: prep_coupling(cv.at[after], bn, k) for k in range(5)],
        )
        keyed = [((i + 0.5) / len(q), f) for q in seqs for i, f in enumerate(q)]
        for _, f in sorted(keyed, key=lambda z: z[0]):
            f()

        @pl.when(p > 0)
        def _():
            patch_out(before).start()

    def pair(h, carry):
        stage(2 * h, 0)
        stage(2 * h + 1, 1)
        return carry

    for i in range(2):
        for c in range(6):
            prep_field(uv.at[i], bufs[i][0], c)
        for k in range(3):
            prep_left(tv.at[i], bufs[i][1], k)
    for k in range(5):
        prep_coupling(cv.at[0], b0, k)
    left_products(t0, u0, p0)
    half = n // 4
    lax.fori_loop(0, half, pair, 0)

    settle(sbuf, rbuf, 0)

    def slots_of(buf):
        for k in range(2):
            for c in range(6):
                h, l = split(buf[:, k * 6 + c, :])
                cols = slice(c * 128, c * 128 + 128)
                acat[k * 256 : k * 256 + 128, cols] = h
                acat[k * 256 + 128 : k * 256 + 256, cols] = l

    slots_of(rbuf)
    strip = dot(taker[...], acat[...])

    def taps(x, start, count, rows):
        total = None
        for tap in range(start, start + count):
            v = jnp.take_along_axis(x, idx[tap, rows, :], axis=1) * wts[tap, rows, :]
            total = v if total is None else total + v
        return total

    own = n * 4
    first_rows, second_rows = slice(0, own), slice(own, 2 * own)
    tr_a, tr_b = [], []
    for c in range(6):
        cols = slice(c * 128, c * 128 + 128)
        tr_a.append(taps(strip[0:own, cols], 0, 3, first_rows))
        tr_b.append(taps(strip[own : 2 * own, cols], 0, 3, second_rows))
    ang = angles[...]
    cosv, sinv = jnp.cos(ang), jnp.sin(ang)
    ca, cb_, cg = (cosv[:, k : k + 1] for k in range(3))
    sa, sb, sg = (sinv[:, k : k + 1] for k in range(3))
    rot = (
        (cg * cb_, cg * sb * sa - sg * ca, cg * sb * ca + sg * sa),
        (sg * cb_, sg * sb * sa + cg * ca, sg * sb * ca - cg * sa),
        (-sb, cb_ * sa, cb_ * ca),
    )
    for blk in range(2):
        pen = penalty[:, blk, :]
        load = []
        for c in range(3):
            turned = sum(rot[c][d] * tr_b[3 * blk + d] for d in range(3))
            load.append(pen * (tr_a[3 * blk + c] - turned))
        for c in range(3):
            back = -sum(rot[d][c] * load[d] for d in range(3))
            cols = slice((3 * blk + c) * 128, (3 * blk + c) * 128 + 128)
            for x, rows in ((load[c], first_rows), (back, second_rows)):
                h, l = split(taps(x, 3, 6, rows))
                acat[rows, cols] = h
                acat[128 + rows.start : 128 + rows.stop, cols] = l
    for k in range(2):
        slots = dot(taker_t[k * 128 : k * 128 + 128, :], acat[0:256, :])
        for c in range(6):
            bbuf[:, k * 6 + c, :] = slots[:, c * 128 : c * 128 + 128]
    exchange(bbuf, fbuf, 1)

    lax.fori_loop(half, n // 2, pair, 0)
    right_products(w1, r1, ov.at[n - 1])
    patch_out(n - 1).start()

    settle(bbuf, fbuf, 1)
    slots_of(fbuf)
    gathered = dot(picker_t[...], acat[...])
    for c in range(6):
        force[:, c, :] = gathered[:, c * 128 : c * 128 + 128]
    pltpu.make_async_copy(ov, part_hbm, out_sem).wait()


def add_kernel(part_hbm, force, out_hbm, buf, in_sem, out_sem):
    n = buf.shape[0]

    def fetch(p):
        return pltpu.make_async_copy(part_hbm.at[p], buf.at[p], in_sem.at[p])

    def put(p):
        return pltpu.make_async_copy(buf.at[p], out_hbm.at[p], out_sem)

    def begin(p, carry):
        fetch(p).start()
        return carry

    lax.fori_loop(0, n, begin, 0)
    lane = iota((8, 128), 1)
    sub = iota((8, 128), 0)
    left = jnp.where(lane == 0, 1.5, jnp.where(lane == 1, -0.5, 0.0))
    right = jnp.where(lane == 127, 1.5, jnp.where(lane == 126, -0.5, 0.0))
    spread = jnp.where(sub < 2, left, jnp.where(sub < 4, right, 0.0)).astype(BF)
    top = jnp.where(sub == 0, 1.5, jnp.where(sub == 1, -0.5, 0.0))
    bottom = jnp.where(sub == 7, 1.5, jnp.where(sub == 6, -0.5, 0.0))

    def one(p, carry):
        fetch(p).wait()
        for c in range(6):
            f0 = force[p, c : c + 1, :]
            f1 = force[n + p, c : c + 1, :]
            f2 = force[2 * n + p, c : c + 1, :]
            f3 = force[3 * n + p, c : c + 1, :]
            h2, l2 = f2.astype(BF).astype(F32), f2 - f2.astype(BF).astype(F32)
            h3, l3 = f3.astype(BF).astype(F32), f3 - f3.astype(BF).astype(F32)
            rows = jnp.where(
                sub == 0, h2, jnp.where(sub == 1, l2, jnp.where(sub == 2, h3, jnp.where(sub == 3, l3, 0.0)))
            ).astype(BF)
            cells = lax.dot_general(
                rows, spread, (((0,), (0,)), ((), ())), preferred_element_type=F32
            )
            buf[p, c] = buf[p, c] + cells
            buf[p, c, 0:8, :] = buf[p, c, 0:8, :] + top * f0
            buf[p, c, 120:128, :] = buf[p, c, 120:128, :] + bottom * f1
        put(p).start()
        return carry

    lax.fori_loop(0, n, one, 0)
    pltpu.make_async_copy(buf, out_hbm, out_sem).wait()


def shards(devs, inner, patch_field, patch_tables, coupling, side_device, side_detail, penalty, angles):
    n = patch_field.shape[0]
    rid = side_detail[:, 1] * n + side_detail[:, 0]
    code = ((rid * 32 + side_detail[:, 2]) * 128 + side_detail[:, 3]) * 128 + side_device[:, 0]
    code = code.reshape(devs, 128)
    anyspec = pl.BlockSpec(memory_space=pl.ANY)
    vspec = pl.BlockSpec(memory_space=pltpu.VMEM)
    v = pltpu.VMEM
    big = v(patch_field.shape, F32)
    wire = v((devs, 12, 128), F32)
    dma = pltpu.SemaphoreType.DMA
    part, force = pl.pallas_call(
        functools.partial(main_kernel, devs, inner),
        out_shape=(
            jax.ShapeDtypeStruct(patch_field.shape, F32),
            jax.ShapeDtypeStruct((4 * n, 6, 128), F32),
        ),
        in_specs=[vspec] * 3 + [anyspec] * 3,
        out_specs=(anyspec, vspec),
        scratch_shapes=[big, big, v(coupling.shape, F32), big]
        + [v((384, 768), BF)] * 2
        + [v((384, 384), BF)] * 2
        + [v((256, 384), BF)] * 2
        + [v((384, 768), F32)] * 2
        + [v((768, 768), BF)] * 2
        + [v((30, 6, 128), F32)] * 2
        + [
            v((64, 6, 128), F32),
            v((128, 768), BF),
            v((512, 768), BF),
            v((256, 128), BF),
            v((64, 512), BF),
            v((128, 512), BF),
            v((256, 256), BF),
            v((9, 128, 128), F32),
            v((9, 128, 128), jnp.int32),
        ]
        + [wire] * 4
        + [dma((9,)), dma, dma((2,)), dma((2,)), dma((2,))],
        compiler_params=pltpu.CompilerParams(
            collective_id=0, has_side_effects=True, vmem_limit_bytes=50 * 2**20
        ),
    )(code, penalty, angles, patch_field, patch_tables, coupling)
    return pl.pallas_call(
        add_kernel,
        out_shape=jax.ShapeDtypeStruct(patch_field.shape, F32),
        in_specs=[anyspec, vspec],
        out_specs=anyspec,
        scratch_shapes=[big, dma((n,)), dma],
        compiler_params=pltpu.CompilerParams(vmem_limit_bytes=16 * 2**20),
    )(part, force)


def solution(mesh):
    devs = mesh.shape["chip"] * mesh.shape["cores"]
    return jax.shard_map(
        functools.partial(shards, devs, mesh.shape["cores"]),
        mesh=mesh,
        in_specs=(
            P(("chip", "cores"), None, None, None),
            P(("chip", "cores"), None, None, None),
            P(("chip", "cores"), None, None, None),
            P(),
            P(),
            P(("chip", "cores"), None, None),
            P(("chip", "cores"), None),
        ),
        out_specs=P(("chip", "cores"), None, None, None),
        check_vma=False,
    )
```

```python
import functools

import jax
import jax.numpy as jnp
from jax import lax
from jax.experimental import pallas as pl
from jax.experimental.pallas import tpu as pltpu
from jax.sharding import PartitionSpec as P

BF = jnp.bfloat16
F32 = jnp.float32
MESH = pl.DeviceIdType.MESH
CH = 16
TABLES = ((0, 0, None), (1, 3, (1, 1)), (2, 4, (2, 2)))


def split(x):
    high = x.astype(BF)
    return high, (x - high.astype(F32)).astype(BF)


def dot(a, b):
    return lax.dot_general(a, b, (((1,), (0,)), ((), ())), preferred_element_type=F32)


def dot_t(a, b):
    return lax.dot_general(a, b, (((1,), (1,)), ((), ())), preferred_element_type=F32)


def prep_field(field, ucat, c):
    h, l = split(field[c])
    cols = slice(c * 128, c * 128 + 128)
    ucat[0:128, cols] = h
    ucat[128:256, cols] = l
    ucat[256:384, cols] = h


def prep_left(tables, tcat, t):
    h, l = split(tables[t])
    rows = slice(t * 128, t * 128 + 128)
    tcat[rows, 0:128] = h
    tcat[rows, 128:256] = h
    tcat[rows, 256:384] = l


def prep_right(tables, rcat, s):
    h, l = split(tables[(4, 3, 5)[s]])
    cols = slice(s * 128, s * 128 + 128)
    rcat[0:128, cols] = h
    rcat[128:256, cols] = l


def prep_coupling(coup, cb, t, c):
    tile = coup[t, c]
    row = (t * 6 + c) * 8
    for p in range(cb.shape[0]):
        cb[p, row : row + 6, :] = jnp.broadcast_to(tile[:, p : p + 1], (6, 128))


def left_products(tcat, ucat, prod):
    prod[...] = dot(tcat[...], ucat[...])


def right_products(mixed, rcat, out):
    o = dot_t(mixed[:, 0:384], rcat[...])
    o2 = dot_t(mixed[:, 384:768], rcat[0:128, :])
    for c in range(6):
        q = slice(c * 128, c * 128 + 128)
        out[c] = (o[q, 0:128] + o[q, 128:256]) + o2[q]


def mix(prod, cb, mixed, r):
    def put(s, c, acc):
        h, l = split(acc)
        rows = slice(c * 128 + r, c * 128 + r + CH)
        mixed[rows, s * 128 : s * 128 + 128] = h
        mixed[rows, 384 + s * 128 : 384 + s * 128 + 128] = l

    def coef(t, c, d):
        row = (t * 6 + c) * 8 + d
        return jnp.broadcast_to(cb[row : row + 1, :], (CH, 128))

    main = [None] * 6
    for t, term, other in TABLES:
        side = [None] * 6
        for d in range(6):
            x = prod[t * 128 + r : t * 128 + r + CH, d * 128 : d * 128 + 128]
            for c in range(6):
                v = x * coef(term, c, d)
                main[c] = v if main[c] is None else main[c] + v
                if other:
                    v = x * coef(other[0], c, d)
                    side[c] = v if side[c] is None else side[c] + v
        if other:
            for c in range(6):
                put(other[1], c, side[c])
    for c in range(6):
        put(0, c, main[c])


def spline(v):
    m = jnp.abs(v)
    far = jnp.maximum(1.5 - m, 0.0)
    return jnp.where(m < 0.5, 0.75 - m * m, 0.5 * far * far)


def iota(shape, axis):
    return lax.broadcasted_iota(jnp.int32, shape, axis)


def main_kernel(
    devs, side, inner, device_hbm, detail_hbm, penalty_hbm, angles_hbm, field_hbm, tables_hbm, coup_hbm, ov, force,
    uv, tv, cv, u0, u1, t0, t1, r0, r1, p0, p1, w0, w1, cb,
    device, detail, penalty, angles, comb, ccat, acat, picker, picker_t, taker, taker_t, wts, idx, sbuf, rbuf, bbuf, fbuf,
    in_sem, send_sem, recv_sem, self_sem,
):
    n = uv.shape[0]
    me = lax.axis_index(("chip", "cores"))

    chip_me, core_me = me // inner, me % inner
    my_x, my_y = chip_me // (side * side), chip_me // side % side
    my_zs = [lax.rem(chip_me + k, side) for k in range(side)]
    my_cores = [lax.rem(core_me + k, inner) for k in range(inner)]
    order_z = [side // 2] + [k for k in range(side) if k != side // 2][::-1]

    def for_others(action):
        def line(i, carry):
            y = lax.rem(i // side + side // 2, side)
            x = lax.rem(i + y, side)
            base = (lax.rem(my_x + x, side) * side + lax.rem(my_y + y, side)) * side
            for k in order_z:
                for core in range(inner):
                    who = (base + my_zs[k], my_cores[core])
                    if k == 0 and core == 0:
                        pl.when((x > 0) | (y > 0))(functools.partial(action, who))
                    else:
                        action(who)
            return carry

        lax.fori_loop(0, side * side, line, 0)

    barrier = pltpu.get_barrier_semaphore()
    for_others(
        lambda who: pl.semaphore_signal(barrier, inc=1, device_id=who, device_id_type=MESH)
    )

    groups = 4
    per = n // groups
    loads_u = [
        pltpu.make_async_copy(
            field_hbm.at[pl.ds(g * per, per)], uv.at[pl.ds(g * per, per)], in_sem.at[g]
        )
        for g in range(groups)
    ]
    loads_t = [
        pltpu.make_async_copy(
            tables_hbm.at[pl.ds(g * per, per)], tv.at[pl.ds(g * per, per)], in_sem.at[groups + g]
        )
        for g in range(groups)
    ]
    small = [
        pltpu.make_async_copy(src, dst, in_sem.at[2 * groups + i])
        for i, (src, dst) in enumerate(
            ((device_hbm, device), (detail_hbm, detail), (penalty_hbm, penalty), (angles_hbm, angles), (coup_hbm, cv))
        )
    ]
    for copy in small[0:2] + loads_u + small[2:] + loads_t:
        copy.start()

    small[0].wait()
    small[1].wait()
    lane = iota((128, 128), 1)
    sub = iota((128, 128), 0)
    lane_f = lane.astype(F32)
    sub_f = sub.astype(F32)
    eye = lane == sub
    hit = device[...] == me
    rid = (detail[:, 1, :] * n + detail[:, 0, :]).astype(F32)
    first = jnp.min(jnp.where(hit, lane_f, 1e6), axis=1, keepdims=True)
    last = jnp.max(jnp.where(hit, lane_f, -1.0), axis=1, keepdims=True)
    row0 = jnp.sum(jnp.where(lane_f == first, rid, 0.0), axis=1, keepdims=True)
    row1 = jnp.sum(jnp.where(lane_f == last, rid, 0.0), axis=1, keepdims=True)
    row0 = jnp.where(last >= 0.0, row0, -1.0)
    row1 = jnp.where(last > first, row1, -1.0)

    def to_row(col):
        return jnp.sum(jnp.where(eye, col, 0.0), axis=0, keepdims=True)

    def one_hot(mask):
        return jnp.where(mask, 1.0, 0.0).astype(BF)

    edge_lane = (lane & 63).astype(F32)
    edge_sub = iota((64, 128), 0).astype(F32)
    for k, row in enumerate((row0, row1)):
        picker[k * 128 : k * 128 + 128, :] = one_hot(row == edge_lane)
        flat = one_hot(to_row(row) == edge_sub)
        picker_t[:, k * 256 : k * 256 + 128] = flat
        picker_t[:, k * 256 + 128 : k * 256 + 256] = flat

    dev_row = device[pl.ds(me, 1), :].astype(F32)
    ln_row = detail[me, 3:4, :].astype(F32)
    st_row = detail[me, 2:3, :].astype(F32)
    order = jnp.where(sub < 64, 2 * sub, 2 * sub - 127)
    perm = lane == order

    def to_col(row):
        return jnp.sum(jnp.where(perm, row, 0.0), axis=1, keepdims=True)

    dev_col, ln, st = to_col(dev_row), to_col(ln_row), to_col(st_row)
    slot = jnp.sum(
        jnp.where((dev_row == dev_col) & (lane < order), 1.0, 0.0), axis=1, keepdims=True
    )
    dev_flat, slot_flat = to_row(dev_col), to_row(slot)
    for k in range(2):
        t = one_hot((lane_f == dev_col) & (slot == float(k)))
        taker[:, k * 256 : k * 256 + 128] = t
        taker[:, k * 256 + 128 : k * 256 + 256] = t
        t = one_hot((sub_f == dev_flat) & (slot_flat == float(k)))
        taker_t[k * 128 : k * 128 + 128, 0:128] = t
        taker_t[k * 128 : k * 128 + 128, 128:256] = t

    def strips(p, carry):
        cols = None
        for c in range(6):
            x = uv[p, c]
            comb[p, c : c + 1, :] = 1.5 * x[0:1] - 0.5 * x[1:2]
            comb[n + p, c : c + 1, :] = 1.5 * x[127:128] - 0.5 * x[126:127]
            x = pltpu.roll(x, 2 + 4 * c, 1)
            cols = x if cols is None else jnp.where(lane < 4 * c, cols, x)
        y = jnp.transpose(cols[:, 0:24])
        for c in range(6):
            y0, y1, y2, y3 = (y[4 * c + k : 4 * c + k + 1] for k in range(4))
            comb[2 * n + p, c : c + 1, :] = 1.5 * y2 - 0.5 * y3
            comb[3 * n + p, c : c + 1, :] = 1.5 * y1 - 0.5 * y0
        return carry

    for g in range(groups):
        loads_u[g].wait()
        lax.fori_loop(g * per, (g + 1) * per, strips, 0)
    for c in range(6):
        h, l = split(comb[:, c, :])
        ccat[0:64, c * 128 : c * 128 + 128] = h
        ccat[64:128, c * 128 : c * 128 + 128] = l
    for k in range(2):
        slots = dot(picker[k * 128 : k * 128 + 128, :], ccat[...])
        for c in range(6):
            sbuf[k * 6 + c] = slots[:, c * 128 : c * 128 + 128]
    pl.semaphore_wait(barrier, devs - 1)

    def exchange(src, dst, which):
        def send(who):
            pltpu.make_async_remote_copy(
                src_ref=src.at[:, who[0] * inner + who[1], :],
                dst_ref=dst.at[:, me, :],
                send_sem=send_sem.at[which],
                recv_sem=recv_sem.at[which],
                device_id=who,
                device_id_type=MESH,
            ).start()

        for_others(send)
        pltpu.make_async_copy(src.at[:, me, :], dst.at[:, me, :], self_sem.at[which]).start()

    def settle(src, dst, which):
        others = pl.ds(0, devs - 1)
        for sem in (send_sem, recv_sem):
            pltpu.make_async_copy(src.at[:, others, :], dst.at[:, others, :], sem.at[which]).wait()
        pltpu.make_async_copy(src.at[:, me, :], dst.at[:, me, :], self_sem.at[which]).wait()

    exchange(sbuf, rbuf, 0)

    unit = st * 256.0 + (2.0 * lane_f + 1.0) * ln
    near = jnp.floor((unit + 128.0) * (1.0 / 256.0))
    for tap in range(3):
        j = near + float(tap - 1)
        w = spline(unit * (1.0 / 256.0) - j)
        wts[tap] = jnp.where((j >= 0.0) & (j <= 127.0), w, 0.0)
        idx[tap] = jnp.clip(j, 0.0, 127.0).astype(jnp.int32)
    low = jnp.floor(((256.0 * (lane_f - st) - 384.0) / ln - 1.0) * 0.5) + 1.0
    for tap in range(6):
        q = low + float(tap)
        v = (st * 256.0 + (2.0 * q + 1.0) * ln) * (1.0 / 256.0) - lane_f
        wts[3 + tap] = jnp.where((q >= 0.0) & (q <= 127.0), spline(v), 0.0)
        idx[3 + tap] = jnp.clip(q, 0.0, 127.0).astype(jnp.int32)

    bufs = ((u0, t0, r0, p0, w0), (u1, t1, r1, p1, w1))
    small[4].wait()
    for t in range(5):
        for c in range(6):
            prep_coupling(cv, cb, t, c)
    for copy in loads_t:
        copy.wait()

    def stage(p, j):
        u, t, r, pr, w = bufs[j]
        un, tn, rn, prn, wn = bufs[1 - j]
        before = jnp.maximum(p - 1, 0)
        later = jnp.minimum(p + 2, n - 1)
        seqs = (
            [lambda k=k: mix(pr, cb.at[p], w, k * CH) for k in range(128 // CH)],
            [
                lambda: left_products(tn, un, prn),
                lambda: right_products(wn, rn, ov.at[before]),
            ],
            [lambda c=c: prep_field(uv.at[later], u, c) for c in range(6)]
            + [lambda k=k: prep_left(tv.at[later], t, k) for k in range(3)]
            + [lambda k=k: prep_right(tv.at[p], r, k) for k in range(3)],
        )
        keyed = [((i + 0.5) / len(q), f) for q in seqs for i, f in enumerate(q)]
        for _, f in sorted(keyed, key=lambda z: z[0]):
            f()

    def pair(h, carry):
        stage(2 * h, 0)
        stage(2 * h + 1, 1)
        return carry

    for i in range(2):
        for c in range(6):
            prep_field(uv.at[i], bufs[i][0], c)
        for k in range(3):
            prep_left(tv.at[i], bufs[i][1], k)
    left_products(t0, u0, p0)
    half = n // 4
    lax.fori_loop(0, half, pair, 0)

    settle(sbuf, rbuf, 0)

    def slots_of(buf):
        for k in range(2):
            for c in range(6):
                h, l = split(buf[k * 6 + c])
                cols = slice(c * 128, c * 128 + 128)
                acat[k * 256 : k * 256 + 128, cols] = h
                acat[k * 256 + 128 : k * 256 + 256, cols] = l

    slots_of(rbuf)
    strip = dot(taker[...], acat[...])

    def taps(x, start, count, rows):
        total = None
        for tap in range(start, start + count):
            v = jnp.take_along_axis(x, idx[tap, rows, :], axis=1) * wts[tap, rows, :]
            total = v if total is None else total + v
        return total

    own = n * 4
    first_rows, second_rows = slice(0, own), slice(own, 2 * own)
    tr_a, tr_b = [], []
    for c in range(6):
        cols = slice(c * 128, c * 128 + 128)
        tr_a.append(taps(strip[0:own, cols], 0, 3, first_rows))
        tr_b.append(taps(strip[own : 2 * own, cols], 0, 3, second_rows))
    small[2].wait()
    small[3].wait()
    half_eye = iota((own, own), 0) == iota((own, own), 1)
    ang = jnp.concatenate(
        [
            jnp.sum(jnp.where(half_eye, angles[k : k + 1, :], 0.0), axis=1, keepdims=True)
            for k in range(3)
        ],
        axis=1,
    )
    cosv, sinv = jnp.cos(ang), jnp.sin(ang)
    ca, cb_, cg = (cosv[:, k : k + 1] for k in range(3))
    sa, sb, sg = (sinv[:, k : k + 1] for k in range(3))
    rot = (
        (cg * cb_, cg * sb * sa - sg * ca, cg * sb * ca + sg * sa),
        (sg * cb_, sg * sb * sa + cg * ca, sg * sb * ca - cg * sa),
        (-sb, cb_ * sa, cb_ * ca),
    )
    for blk in range(2):
        pen = penalty[:, blk, :]
        load = []
        for c in range(3):
            turned = sum(rot[c][d] * tr_b[3 * blk + d] for d in range(3))
            load.append(pen * (tr_a[3 * blk + c] - turned))
        for c in range(3):
            back = -sum(rot[d][c] * load[d] for d in range(3))
            cols = slice((3 * blk + c) * 128, (3 * blk + c) * 128 + 128)
            for x, rows in ((load[c], first_rows), (back, second_rows)):
                h, l = split(taps(x, 3, 6, rows))
                acat[rows, cols] = h
                acat[128 + rows.start : 128 + rows.stop, cols] = l
    for k in range(2):
        slots = dot(taker_t[k * 128 : k * 128 + 128, :], acat[0:256, :])
        for c in range(6):
            bbuf[k * 6 + c] = slots[:, c * 128 : c * 128 + 128]
    exchange(bbuf, fbuf, 1)

    lax.fori_loop(half, n // 2, pair, 0)
    right_products(w1, r1, ov.at[n - 1])

    settle(bbuf, fbuf, 1)
    slots_of(fbuf)
    gathered = dot(picker_t[...], acat[...])
    for c in range(6):
        force[:, c, :] = gathered[:, c * 128 : c * 128 + 128]


def add_kernel(part, force, out_hbm, buf, out_sem):
    n = buf.shape[0]

    def put(p):
        return pltpu.make_async_copy(buf.at[p], out_hbm.at[p], out_sem)

    lane = iota((8, 128), 1)
    sub = iota((8, 128), 0)
    left = jnp.where(lane == 0, 1.5, jnp.where(lane == 1, -0.5, 0.0))
    right = jnp.where(lane == 127, 1.5, jnp.where(lane == 126, -0.5, 0.0))
    spread = jnp.where(sub < 2, left, jnp.where(sub < 4, right, 0.0)).astype(BF)
    top = jnp.where(sub == 0, 1.5, jnp.where(sub == 1, -0.5, 0.0))
    bottom = jnp.where(sub == 7, 1.5, jnp.where(sub == 6, -0.5, 0.0))

    def one(p, carry):
        for c in range(6):
            f0 = force[p, c : c + 1, :]
            f1 = force[n + p, c : c + 1, :]
            f2 = force[2 * n + p, c : c + 1, :]
            f3 = force[3 * n + p, c : c + 1, :]
            h2, l2 = f2.astype(BF).astype(F32), f2 - f2.astype(BF).astype(F32)
            h3, l3 = f3.astype(BF).astype(F32), f3 - f3.astype(BF).astype(F32)
            rows = jnp.where(
                sub == 0, h2, jnp.where(sub == 1, l2, jnp.where(sub == 2, h3, jnp.where(sub == 3, l3, 0.0)))
            ).astype(BF)
            cells = lax.dot_general(
                rows, spread, (((0,), (0,)), ((), ())), preferred_element_type=F32
            )
            buf[p, c] = part[p, c] + cells
            buf[p, c, 0:8, :] = buf[p, c, 0:8, :] + top * f0
            buf[p, c, 120:128, :] = buf[p, c, 120:128, :] + bottom * f1
        put(p).start()
        return carry

    lax.fori_loop(0, n, one, 0)
    pltpu.make_async_copy(buf, out_hbm, out_sem).wait()


def shards(devs, side, inner, patch_field, patch_tables, coupling, side_device, side_detail, penalty, angles):
    n = patch_field.shape[0]
    detail = side_detail.reshape(devs, 128, 4).transpose(0, 2, 1)
    device = side_device.reshape(devs, 128)
    coup = coupling.transpose(1, 2, 3, 0)
    anyspec = pl.BlockSpec(memory_space=pltpu.HBM)
    vspec = pl.BlockSpec(memory_space=pltpu.VMEM)
    v = pltpu.VMEM
    big = v(patch_field.shape, F32)
    wire = v((12, devs, 128), F32)
    dma = pltpu.SemaphoreType.DMA
    part, force = pl.pallas_call(
        functools.partial(main_kernel, devs, side, inner),
        out_shape=(
            jax.ShapeDtypeStruct(patch_field.shape, F32),
            jax.ShapeDtypeStruct((4 * n, 6, 128), F32),
        ),
        in_specs=[anyspec] * 7,
        out_specs=(vspec, vspec),
        scratch_shapes=[big, big, v(coup.shape, F32)]
        + [v((384, 768), BF)] * 2
        + [v((384, 384), BF)] * 2
        + [v((256, 384), BF)] * 2
        + [v((384, 768), F32)] * 2
        + [v((768, 768), BF)] * 2
        + [
            v((n, 240, 128), F32),
            v((devs, 128), jnp.int32),
            v((devs, 4, 128), jnp.int32),
            v(penalty.shape, F32),
            v((3, penalty.shape[0]), F32),
            v((64, 6, 128), F32),
            v((128, 768), BF),
            v((512, 768), BF),
            v((256, 128), BF),
            v((64, 512), BF),
            v((128, 512), BF),
            v((256, 256), BF),
            v((9, 128, 128), F32),
            v((9, 128, 128), jnp.int32),
        ]
        + [wire] * 4
        + [dma((13,)), dma((2,)), dma((2,)), dma((2,))],
        compiler_params=pltpu.CompilerParams(
            collective_id=0, has_side_effects=True, vmem_limit_bytes=47 * 2**20
        ),
    )(device, detail, penalty, angles.T, patch_field, patch_tables, coup)
    return pl.pallas_call(
        add_kernel,
        out_shape=jax.ShapeDtypeStruct(patch_field.shape, F32),
        in_specs=[vspec, vspec],
        out_specs=anyspec,
        scratch_shapes=[big, dma],
        compiler_params=pltpu.CompilerParams(vmem_limit_bytes=16 * 2**20),
    )(part, force)


def solution(mesh):
    devs = mesh.shape["chip"] * mesh.shape["cores"]
    return jax.shard_map(
        functools.partial(shards, devs, round(mesh.shape["chip"] ** (1 / 3)), mesh.shape["cores"]),
        mesh=mesh,
        in_specs=(
            P(("chip", "cores"), None, None, None),
            P(("chip", "cores"), None, None, None),
            P(("chip", "cores"), None, None, None),
            P(),
            P(),
            P(("chip", "cores"), None, None),
            P(("chip", "cores"), None),
        ),
        out_specs=P(("chip", "cores"), None, None, None),
        check_vma=False,
    )
```

```python
import functools

import jax
import jax.numpy as jnp
from jax import lax
from jax.experimental import pallas as pl
from jax.experimental.pallas import tpu as pltpu
from jax.sharding import PartitionSpec as P

BF = jnp.bfloat16
F32 = jnp.float32
MESH = pl.DeviceIdType.MESH
WIDTH = 4


def split(x):
    high = x.astype(BF)
    return high, (x - high.astype(F32)).astype(BF)


def dot(a, b):
    return lax.dot_general(a, b, (((1,), (0,)), ((), ())), preferred_element_type=F32)


def dot_t(a, b):
    return lax.dot_general(a, b, (((1,), (1,)), ((), ())), preferred_element_type=F32)


def prep_field(field, ucat, c):
    h, l = split(field[c])
    cols = slice(c * 128, c * 128 + 128)
    ucat[0:128, cols] = h
    ucat[128:256, cols] = l
    ucat[256:384, cols] = h


def prep_left(tables, tcat, t):
    h, l = split(tables[t])
    rows = slice(t * 128, t * 128 + 128)
    tcat[rows, 0:128] = h
    tcat[rows, 128:256] = h
    tcat[rows, 256:384] = l


def prep_right(tables, rcat, s):
    h, l = split(tables[(4, 3, 5)[s]])
    cols = slice(s * 128, s * 128 + 128)
    rcat[0:128, cols] = h
    rcat[128:256, cols] = l


def prep_coupling(coup, cb, t, c):
    tile = jnp.concatenate([coup[t, c], jnp.zeros((2, coup.shape[3]), F32)], axis=0)
    row = (t * 6 + c) * 8
    for p in range(cb.shape[0]):
        cb[p, row : row + 8, :] = jnp.broadcast_to(tile[:, p : p + 1], (8, 128))


def left_products(tcat, ucat, prod, m):
    cols = slice(m * 256, m * 256 + 256)
    prod[:, cols] = dot(tcat[...], ucat[:, cols])


def right_products(mixed, rcat, out):
    o = dot_t(mixed[:, 0:384], rcat[...])
    o2 = dot_t(mixed[:, 384:768], rcat[0:128, :])
    for c in range(6):
        q = slice(c * 128, c * 128 + 128)
        out[c] = (o[q, 0:128] + o[q, 128:256]) + o2[q]


def kron_constants(select, high_mask, low_mask, diag):
    row, col = iota(select.shape, 0) // 8, iota(select.shape, 1) // 8
    kind, term = row // 6, col // 6
    used = ((kind == 0) & ((term == 0) | (term >= 3))) | ((kind > 0) & (term == kind))
    select[...] = jnp.where(used & (row % 6 == col % 6), 1.0, 0.0).astype(BF)
    row, col = iota(high_mask.shape, 0), iota(high_mask.shape, 1) // 8
    term, d = row // 48, row % 8
    table = jnp.where(term >= 3, term - 2, term)
    part, block = col // 18, col % 18
    match = (table == block // 6) & (d == block % 6)
    high_mask[...] = jnp.where(match & (part < 2), 1.0, 0.0).astype(BF)
    low_mask[...] = jnp.where(match & (part == 2), 1.0, 0.0).astype(BF)
    row, col = iota(diag.shape, 0), iota(diag.shape, 1)
    diag[...] = jnp.where(row % 8 == col % 8, 1.0, 0.0)


def make_kron(cb, select, high_mask, low_mask, diag, kron):
    h, l = split(cb[...])
    parts = []
    for k in range(0, 432, 128):
        n = min(128, 432 - k)
        cols = slice(k, k + n)
        parts.append(h[:, 0:n] * high_mask[:, cols] + l[:, 0:n] * low_mask[:, cols])
    kron[...] = (dot(select[...], jnp.concatenate(parts, axis=1)) * diag[...]).astype(BF)


def stack_products(prod, pk, m):
    t, d = m // 3, 2 * (m % 3)
    for r in range(16):
        rows = slice(t * 128 + 8 * r, t * 128 + 8 * r + 8)
        x = jnp.concatenate(
            [prod[rows, d * 128 : d * 128 + 128], prod[rows, d * 128 + 128 : d * 128 + 256]], axis=0
        )
        h, l = split(x)
        cols = slice(r * 128, r * 128 + 128)
        pk[16 * m : 16 * m + 16, cols] = h
        pk[144 + 16 * m : 160 + 16 * m, cols] = l
        pk[288 + 16 * m : 304 + 16 * m, cols] = h


def stack(prod, pk, m):
    for t in range(3):
        stack_products(prod, pk, 3 * t + m)


def mix(kron, pk, mixed, m, width):
    o = dot(kron[...], pk[:, m * width * 128 : (m + 1) * width * 128])
    for s in range(3):
        for c in range(6):
            rows = slice((s * 6 + c) * 8, (s * 6 + c) * 8 + 8)
            for r in range(0, width, 2):
                x = jnp.concatenate(
                    [o[rows, r * 128 : r * 128 + 128], o[rows, r * 128 + 128 : r * 128 + 256]], axis=0
                )
                h, l = split(x)
                at = c * 128 + (m * width + r) * 8
                mixed[at : at + 16, s * 128 : s * 128 + 128] = h
                mixed[at : at + 16, 384 + s * 128 : 384 + s * 128 + 128] = l


def spline(v):
    m = jnp.abs(v)
    far = jnp.maximum(1.5 - m, 0.0)
    return jnp.where(m < 0.5, 0.75 - m * m, 0.5 * far * far)


def iota(shape, axis):
    return lax.broadcasted_iota(jnp.int32, shape, axis)


def main_kernel(
    devs, side, inner, device_hbm, detail_hbm, penalty_hbm, angles_hbm, field_hbm, tables_hbm, coup_hbm, ov, force,
    uv, tv, cv, u0, u1, t0, t1, r0, r1, p0, p1, w0, w1, k0, k1, pk0, pk1, select, high_mask, low_mask, diag, cb,
    device, detail, penalty, angles, comb, ccat, acat, picker, picker_t, taker, taker_t, wts, idx, sbuf, rbuf, bbuf, fbuf,
    in_sem, send_sem, recv_sem, self_sem,
):
    n = uv.shape[0]
    me = lax.axis_index(("chip", "cores"))

    chip_me, core_me = me // inner, me % inner
    my_x, my_y = chip_me // (side * side), chip_me // side % side
    my_zs = [lax.rem(chip_me + k, side) for k in range(side)]
    my_cores = [lax.rem(core_me + k, inner) for k in range(inner)]
    order_z = [side // 2] + [k for k in range(side) if k != side // 2][::-1]

    def for_others(action):
        def line(i, carry):
            y = lax.rem(i // side + side // 2, side)
            x = lax.rem(i + y, side)
            base = (lax.rem(my_x + x, side) * side + lax.rem(my_y + y, side)) * side
            for k in order_z:
                for core in range(inner):
                    who = (base + my_zs[k], my_cores[core])
                    if k == 0 and core == 0:
                        pl.when((x > 0) | (y > 0))(functools.partial(action, who))
                    else:
                        action(who)
            return carry

        lax.fori_loop(0, side * side, line, 0)

    barrier = pltpu.get_barrier_semaphore()
    for_others(
        lambda who: pl.semaphore_signal(barrier, inc=1, device_id=who, device_id_type=MESH)
    )

    groups = 4
    per = n // groups
    loads_u = [
        pltpu.make_async_copy(
            field_hbm.at[pl.ds(g * per, per)], uv.at[pl.ds(g * per, per)], in_sem.at[g]
        )
        for g in range(groups)
    ]
    loads_t = [
        pltpu.make_async_copy(
            tables_hbm.at[pl.ds(g * per, per)], tv.at[pl.ds(g * per, per)], in_sem.at[groups + g]
        )
        for g in range(groups)
    ]
    small = [
        pltpu.make_async_copy(src, dst, in_sem.at[2 * groups + i])
        for i, (src, dst) in enumerate(
            ((device_hbm, device), (detail_hbm, detail), (penalty_hbm, penalty), (angles_hbm, angles), (coup_hbm, cv))
        )
    ]
    for copy in small[0:2] + loads_u + small[2:] + loads_t:
        copy.start()

    small[0].wait()
    small[1].wait()
    lane = iota((128, 128), 1)
    sub = iota((128, 128), 0)
    lane_f = lane.astype(F32)
    sub_f = sub.astype(F32)
    eye = lane == sub
    hit = device[...] == me
    rid = (detail[:, 1, :] * n + detail[:, 0, :]).astype(F32)
    first = jnp.min(jnp.where(hit, lane_f, 1e6), axis=1, keepdims=True)
    last = jnp.max(jnp.where(hit, lane_f, -1.0), axis=1, keepdims=True)
    row0 = jnp.sum(jnp.where(lane_f == first, rid, 0.0), axis=1, keepdims=True)
    row1 = jnp.sum(jnp.where(lane_f == last, rid, 0.0), axis=1, keepdims=True)
    row0 = jnp.where(last >= 0.0, row0, -1.0)
    row1 = jnp.where(last > first, row1, -1.0)

    def to_row(col):
        return jnp.sum(jnp.where(eye, col, 0.0), axis=0, keepdims=True)

    def one_hot(mask):
        return jnp.where(mask, 1.0, 0.0).astype(BF)

    edge_lane = (lane & 63).astype(F32)
    edge_sub = iota((64, 128), 0).astype(F32)
    for k, row in enumerate((row0, row1)):
        picker[k * 128 : k * 128 + 128, :] = one_hot(row == edge_lane)
        flat = one_hot(to_row(row) == edge_sub)
        picker_t[:, k * 256 : k * 256 + 128] = flat
        picker_t[:, k * 256 + 128 : k * 256 + 256] = flat

    dev_row = device[pl.ds(me, 1), :].astype(F32)
    ln_row = detail[me, 3:4, :].astype(F32)
    st_row = detail[me, 2:3, :].astype(F32)
    order = jnp.where(sub < 64, 2 * sub, 2 * sub - 127)
    perm = lane == order

    def to_col(row):
        return jnp.sum(jnp.where(perm, row, 0.0), axis=1, keepdims=True)

    dev_col, ln, st = to_col(dev_row), to_col(ln_row), to_col(st_row)
    slot = jnp.sum(
        jnp.where((dev_row == dev_col) & (lane < order), 1.0, 0.0), axis=1, keepdims=True
    )
    dev_flat, slot_flat = to_row(dev_col), to_row(slot)
    for k in range(2):
        t = one_hot((lane_f == dev_col) & (slot == float(k)))
        taker[:, k * 256 : k * 256 + 128] = t
        taker[:, k * 256 + 128 : k * 256 + 256] = t
        t = one_hot((sub_f == dev_flat) & (slot_flat == float(k)))
        taker_t[k * 128 : k * 128 + 128, 0:128] = t
        taker_t[k * 128 : k * 128 + 128, 128:256] = t

    def strips(p, carry):
        cols = None
        for c in range(6):
            x = uv[p, c]
            comb[p, c : c + 1, :] = 1.5 * x[0:1] - 0.5 * x[1:2]
            comb[n + p, c : c + 1, :] = 1.5 * x[127:128] - 0.5 * x[126:127]
            x = pltpu.roll(x, 2 + 4 * c, 1)
            cols = x if cols is None else jnp.where(lane < 4 * c, cols, x)
        y = jnp.transpose(cols[:, 0:24])
        for c in range(6):
            y0, y1, y2, y3 = (y[4 * c + k : 4 * c + k + 1] for k in range(4))
            comb[2 * n + p, c : c + 1, :] = 1.5 * y2 - 0.5 * y3
            comb[3 * n + p, c : c + 1, :] = 1.5 * y1 - 0.5 * y0
        return carry

    def strips_pair(i, carry):
        return strips(2 * i + 1, strips(2 * i, carry))

    for g in range(groups):
        loads_u[g].wait()
        lax.fori_loop(g * per // 2, (g + 1) * per // 2, strips_pair, 0)
    for c in range(6):
        h, l = split(comb[:, c, :])
        ccat[0:64, c * 128 : c * 128 + 128] = h
        ccat[64:128, c * 128 : c * 128 + 128] = l
    for k in range(2):
        slots = dot(picker[k * 128 : k * 128 + 128, :], ccat[...])
        for c in range(6):
            sbuf[k * 6 + c] = slots[:, c * 128 : c * 128 + 128]
    pl.semaphore_wait(barrier, devs - 1)

    def exchange(src, dst, which):
        def send(who):
            pltpu.make_async_remote_copy(
                src_ref=src.at[:, who[0] * inner + who[1], :],
                dst_ref=dst.at[:, me, :],
                send_sem=send_sem.at[which],
                recv_sem=recv_sem.at[which],
                device_id=who,
                device_id_type=MESH,
            ).start()

        for_others(send)
        pltpu.make_async_copy(src.at[:, me, :], dst.at[:, me, :], self_sem.at[which]).start()

    def settle(src, dst, which):
        others = pl.ds(0, devs - 1)
        for sem in (send_sem, recv_sem):
            pltpu.make_async_copy(src.at[:, others, :], dst.at[:, others, :], sem.at[which]).wait()
        pltpu.make_async_copy(src.at[:, me, :], dst.at[:, me, :], self_sem.at[which]).wait()

    exchange(sbuf, rbuf, 0)

    unit = st * 256.0 + (2.0 * lane_f + 1.0) * ln
    near = jnp.floor((unit + 128.0) * (1.0 / 256.0))
    for tap in range(3):
        j = near + float(tap - 1)
        w = spline(unit * (1.0 / 256.0) - j)
        wts[tap] = jnp.where((j >= 0.0) & (j <= 127.0), w, 0.0)
        idx[tap] = jnp.clip(j, 0.0, 127.0).astype(jnp.int32)
    low = jnp.floor(((256.0 * (lane_f - st) - 384.0) / ln - 1.0) * 0.5) + 1.0
    for tap in range(6):
        q = low + float(tap)
        v = (st * 256.0 + (2.0 * q + 1.0) * ln) * (1.0 / 256.0) - lane_f
        wts[3 + tap] = jnp.where((q >= 0.0) & (q <= 127.0), spline(v), 0.0)
        idx[3 + tap] = jnp.clip(q, 0.0, 127.0).astype(jnp.int32)

    bufs = ((u0, t0, r0, p0, w0, k0, pk0), (u1, t1, r1, p1, w1, k1, pk1))
    consts = (select, high_mask, low_mask, diag)
    kron_constants(*consts)
    small[4].wait()
    for t in range(5):
        for c in range(6):
            prep_coupling(cv, cb, t, c)
    for copy in loads_t:
        copy.wait()

    def stage(p, j):
        u, t, r, pr, w, kr, pk = bufs[j]
        un, tn, rn, prn, wn, krn, pkn = bufs[1 - j]
        after = jnp.minimum(p + 1, n - 1)
        before = jnp.maximum(p - 1, 0)
        later = jnp.minimum(p + 2, n - 1)
        seqs = (
            [
                lambda: left_products(tn, un, prn, 0),
                lambda: left_products(tn, un, prn, 1),
                lambda: stack(prn, pkn, 0),
                lambda: left_products(tn, un, prn, 2),
                lambda: stack(prn, pkn, 1),
            ]
            + [lambda: mix(kr, pk, w, 0, WIDTH), lambda: stack(prn, pkn, 2)]
            + [lambda k=k: mix(kr, pk, w, k, WIDTH) for k in range(1, 16 // WIDTH)]
            + [
                lambda: right_products(wn, rn, ov.at[before]),
                lambda: make_kron(cb.at[after], *consts, krn),
            ],
            [lambda c=c: prep_field(uv.at[later], u, c) for c in range(6)]
            + [lambda k=k: prep_left(tv.at[later], t, k) for k in range(3)]
            + [lambda k=k: prep_right(tv.at[p], r, k) for k in range(3)],
        )
        keyed = [((i + 0.5) / len(q), f) for q in seqs for i, f in enumerate(q)]
        for _, f in sorted(keyed, key=lambda z: z[0]):
            f()

    def pair(h, carry):
        stage(2 * h, 0)
        stage(2 * h + 1, 1)
        return carry

    for i in range(2):
        for c in range(6):
            prep_field(uv.at[i], bufs[i][0], c)
        for k in range(3):
            prep_left(tv.at[i], bufs[i][1], k)
    for m in range(3):
        left_products(t0, u0, p0, m)
        stack(p0, pk0, m)
    make_kron(cb.at[0], *consts, k0)
    half = n // 4
    lax.fori_loop(0, half, pair, 0)

    settle(sbuf, rbuf, 0)

    def slots_of(buf):
        for k in range(2):
            for c in range(6):
                h, l = split(buf[k * 6 + c])
                cols = slice(c * 128, c * 128 + 128)
                acat[k * 256 : k * 256 + 128, cols] = h
                acat[k * 256 + 128 : k * 256 + 256, cols] = l

    slots_of(rbuf)
    strip = dot(taker[...], acat[...])

    def taps(x, start, count, rows):
        total = None
        for tap in range(start, start + count):
            v = jnp.take_along_axis(x, idx[tap, rows, :], axis=1) * wts[tap, rows, :]
            total = v if total is None else total + v
        return total

    own = n * 4
    first_rows, second_rows = slice(0, own), slice(own, 2 * own)
    tr_a, tr_b = [], []
    for c in range(6):
        cols = slice(c * 128, c * 128 + 128)
        tr_a.append(taps(strip[0:own, cols], 0, 3, first_rows))
        tr_b.append(taps(strip[own : 2 * own, cols], 0, 3, second_rows))
    small[2].wait()
    small[3].wait()
    half_eye = iota((own, own), 0) == iota((own, own), 1)
    ang = jnp.concatenate(
        [
            jnp.sum(jnp.where(half_eye, angles[k : k + 1, :], 0.0), axis=1, keepdims=True)
            for k in range(3)
        ],
        axis=1,
    )
    cosv, sinv = jnp.cos(ang), jnp.sin(ang)
    ca, cb_, cg = (cosv[:, k : k + 1] for k in range(3))
    sa, sb, sg = (sinv[:, k : k + 1] for k in range(3))
    rot = (
        (cg * cb_, cg * sb * sa - sg * ca, cg * sb * ca + sg * sa),
        (sg * cb_, sg * sb * sa + cg * ca, sg * sb * ca - cg * sa),
        (-sb, cb_ * sa, cb_ * ca),
    )
    for blk in range(2):
        pen = penalty[:, blk, :]
        load = []
        for c in range(3):
            turned = sum(rot[c][d] * tr_b[3 * blk + d] for d in range(3))
            load.append(pen * (tr_a[3 * blk + c] - turned))
        for c in range(3):
            back = -sum(rot[d][c] * load[d] for d in range(3))
            cols = slice((3 * blk + c) * 128, (3 * blk + c) * 128 + 128)
            for x, rows in ((load[c], first_rows), (back, second_rows)):
                h, l = split(taps(x, 3, 6, rows))
                acat[rows, cols] = h
                acat[128 + rows.start : 128 + rows.stop, cols] = l
    for k in range(2):
        slots = dot(taker_t[k * 128 : k * 128 + 128, :], acat[0:256, :])
        for c in range(6):
            bbuf[k * 6 + c] = slots[:, c * 128 : c * 128 + 128]
    exchange(bbuf, fbuf, 1)

    lax.fori_loop(half, n // 2, pair, 0)
    right_products(w1, r1, ov.at[n - 1])

    settle(bbuf, fbuf, 1)
    slots_of(fbuf)
    gathered = dot(picker_t[...], acat[...])
    for c in range(6):
        force[:, c, :] = gathered[:, c * 128 : c * 128 + 128]


def add_kernel(part, force, out_hbm, buf, out_sem):
    n = buf.shape[0]

    def put(p):
        return pltpu.make_async_copy(buf.at[p], out_hbm.at[p], out_sem)

    lane = iota((8, 128), 1)
    sub = iota((8, 128), 0)
    left = jnp.where(lane == 0, 1.5, jnp.where(lane == 1, -0.5, 0.0))
    right = jnp.where(lane == 127, 1.5, jnp.where(lane == 126, -0.5, 0.0))
    spread = jnp.where(sub < 2, left, jnp.where(sub < 4, right, 0.0)).astype(BF)
    top = jnp.where(sub == 0, 1.5, jnp.where(sub == 1, -0.5, 0.0))
    bottom = jnp.where(sub == 7, 1.5, jnp.where(sub == 6, -0.5, 0.0))

    def one(p, carry):
        for c in range(6):
            f0 = force[p, c : c + 1, :]
            f1 = force[n + p, c : c + 1, :]
            f2 = force[2 * n + p, c : c + 1, :]
            f3 = force[3 * n + p, c : c + 1, :]
            h2, l2 = f2.astype(BF).astype(F32), f2 - f2.astype(BF).astype(F32)
            h3, l3 = f3.astype(BF).astype(F32), f3 - f3.astype(BF).astype(F32)
            rows = jnp.where(
                sub == 0, h2, jnp.where(sub == 1, l2, jnp.where(sub == 2, h3, jnp.where(sub == 3, l3, 0.0)))
            ).astype(BF)
            cells = lax.dot_general(
                rows, spread, (((0,), (0,)), ((), ())), preferred_element_type=F32
            )
            buf[p, c] = part[p, c] + cells
            buf[p, c, 0:8, :] = buf[p, c, 0:8, :] + top * f0
            buf[p, c, 120:128, :] = buf[p, c, 120:128, :] + bottom * f1
        put(p).start()
        return carry

    lax.fori_loop(0, n, one, 0)
    pltpu.make_async_copy(buf, out_hbm, out_sem).wait()


def shards(devs, side, inner, patch_field, patch_tables, coupling, side_device, side_detail, penalty, angles):
    n = patch_field.shape[0]
    detail = side_detail.reshape(devs, 128, 4).transpose(0, 2, 1)
    device = side_device.reshape(devs, 128)
    coup = coupling.transpose(1, 2, 3, 0)
    anyspec = pl.BlockSpec(memory_space=pltpu.HBM)
    vspec = pl.BlockSpec(memory_space=pltpu.VMEM)
    v = pltpu.VMEM
    big = v(patch_field.shape, F32)
    wire = v((12, devs, 128), F32)
    dma = pltpu.SemaphoreType.DMA
    part, force = pl.pallas_call(
        functools.partial(main_kernel, devs, side, inner),
        out_shape=(
            jax.ShapeDtypeStruct(patch_field.shape, F32),
            jax.ShapeDtypeStruct((4 * n, 6, 128), F32),
        ),
        in_specs=[anyspec] * 7,
        out_specs=(vspec, vspec),
        scratch_shapes=[big, big, v(coup.shape, F32)]
        + [v((384, 768), BF)] * 2
        + [v((384, 384), BF)] * 2
        + [v((256, 384), BF)] * 2
        + [v((384, 768), F32)] * 2
        + [v((768, 768), BF)] * 2
        + [v((144, 432), BF)] * 2
        + [
            v((432, 2048), BF),
            v((432, 2048), BF),
            v((144, 240), BF),
            v((240, 432), BF),
            v((240, 432), BF),
            v((144, 432), F32),
            v((n, 240, 128), F32),
            v((devs, 128), jnp.int32),
            v((devs, 4, 128), jnp.int32),
            v(penalty.shape, F32),
            v((3, penalty.shape[0]), F32),
            v((64, 6, 128), F32),
            v((128, 768), BF),
            v((512, 768), BF),
            v((256, 128), BF),
            v((64, 512), BF),
            v((128, 512), BF),
            v((256, 256), BF),
            v((9, 128, 128), F32),
            v((9, 128, 128), jnp.int32),
        ]
        + [wire] * 4
        + [dma((13,)), dma((2,)), dma((2,)), dma((2,))],
        compiler_params=pltpu.CompilerParams(
            collective_id=0, has_side_effects=True, vmem_limit_bytes=47 * 2**20
        ),
    )(device, detail, penalty, angles.T, patch_field, patch_tables, coup)
    return pl.pallas_call(
        add_kernel,
        out_shape=jax.ShapeDtypeStruct(patch_field.shape, F32),
        in_specs=[vspec, vspec],
        out_specs=anyspec,
        scratch_shapes=[big, dma],
        compiler_params=pltpu.CompilerParams(vmem_limit_bytes=16 * 2**20),
    )(part, force)


def solution(mesh):
    devs = mesh.shape["chip"] * mesh.shape["cores"]
    return jax.shard_map(
        functools.partial(shards, devs, round(mesh.shape["chip"] ** (1 / 3)), mesh.shape["cores"]),
        mesh=mesh,
        in_specs=(
            P(("chip", "cores"), None, None, None),
            P(("chip", "cores"), None, None, None),
            P(("chip", "cores"), None, None, None),
            P(),
            P(),
            P(("chip", "cores"), None, None),
            P(("chip", "cores"), None),
        ),
        out_specs=P(("chip", "cores"), None, None, None),
        check_vma=False,
    )
```

```python
import functools

import jax
import jax.numpy as jnp
from jax import lax
from jax.experimental import pallas as pl
from jax.experimental.pallas import tpu as pltpu
from jax.sharding import PartitionSpec as P

BF = jnp.bfloat16
F32 = jnp.float32
MESH = pl.DeviceIdType.MESH
WIDTH = 4


def split(x):
    high = x.astype(BF)
    return high, (x - high.astype(F32)).astype(BF)


def dot(a, b):
    return lax.dot_general(a, b, (((1,), (0,)), ((), ())), preferred_element_type=F32)


def dot_t(a, b):
    return lax.dot_general(a, b, (((1,), (1,)), ((), ())), preferred_element_type=F32)


def prep_field(field, ucat, c):
    h, l = split(field[c])
    cols = slice(c * 128, c * 128 + 128)
    ucat[0:128, cols] = h
    ucat[128:256, cols] = l
    ucat[256:384, cols] = h


def prep_left(tables, tcat, t):
    h, l = split(tables[t])
    rows = slice(t * 128, t * 128 + 128)
    tcat[rows, 0:128] = h
    tcat[rows, 128:256] = h
    tcat[rows, 256:384] = l


def prep_right(tables, rcat, s):
    h, l = split(tables[(4, 3, 5)[s]])
    cols = slice(s * 128, s * 128 + 128)
    rcat[0:128, cols] = h
    rcat[128:256, cols] = l


def prep_coupling(coup, p, cb):
    lane = iota((8, coup.shape[3]), 1)
    for t in range(5):
        for c in range(6):
            tile = jnp.concatenate([coup[t, c], jnp.zeros((2, coup.shape[3]), F32)], axis=0)
            value = jnp.sum(jnp.where(lane == p, tile, 0.0), axis=1, keepdims=True)
            row = (t * 6 + c) * 8
            cb[row : row + 8, :] = jnp.broadcast_to(value, (8, 128))


def left_products(tcat, ucat, prod, m):
    cols = slice(m * 256, m * 256 + 256)
    prod[:, cols] = dot(tcat[...], ucat[:, cols])


def right_products(mixed, rcat, out):
    o = dot_t(mixed[:, 0:384], rcat[...])
    o2 = dot_t(mixed[:, 384:768], rcat[0:128, :])
    for c in range(6):
        q = slice(c * 128, c * 128 + 128)
        out[c] = (o[q, 0:128] + o[q, 128:256]) + o2[q]


def kron_constants(select, high_mask, low_mask, diag):
    row, col = iota(select.shape, 0) // 8, iota(select.shape, 1) // 8
    kind, term = row // 6, col // 6
    used = ((kind == 0) & ((term == 0) | (term >= 3))) | ((kind > 0) & (term == kind))
    select[...] = jnp.where(used & (row % 6 == col % 6), 1.0, 0.0).astype(BF)
    row, col = iota(high_mask.shape, 0), iota(high_mask.shape, 1) // 8
    term, d = row // 48, row % 8
    table = jnp.where(term >= 3, term - 2, term)
    part, block = col // 18, col % 18
    match = (table == block // 6) & (d == block % 6)
    high_mask[...] = jnp.where(match & (part < 2), 1.0, 0.0).astype(BF)
    low_mask[...] = jnp.where(match & (part == 2), 1.0, 0.0).astype(BF)
    row, col = iota(diag.shape, 0), iota(diag.shape, 1)
    diag[...] = jnp.where(row % 8 == col % 8, 1.0, 0.0)


def make_kron(cb, select, high_mask, low_mask, diag, kron):
    h, l = split(cb[...])
    parts = []
    for k in range(0, 432, 128):
        n = min(128, 432 - k)
        cols = slice(k, k + n)
        parts.append(h[:, 0:n] * high_mask[:, cols] + l[:, 0:n] * low_mask[:, cols])
    kron[...] = (dot(select[...], jnp.concatenate(parts, axis=1)) * diag[...]).astype(BF)


def stack_products(prod, pk, m):
    t, d = m // 3, 2 * (m % 3)
    for r in range(16):
        rows = slice(t * 128 + 8 * r, t * 128 + 8 * r + 8)
        x = jnp.concatenate(
            [prod[rows, d * 128 : d * 128 + 128], prod[rows, d * 128 + 128 : d * 128 + 256]], axis=0
        )
        h, l = split(x)
        cols = slice(r * 128, r * 128 + 128)
        pk[16 * m : 16 * m + 16, cols] = h
        pk[144 + 16 * m : 160 + 16 * m, cols] = l
        pk[288 + 16 * m : 304 + 16 * m, cols] = h


def stack(prod, pk, m):
    for t in range(3):
        stack_products(prod, pk, 3 * t + m)


def mix(kron, pk, mixed, m, width):
    o = dot(kron[...], pk[:, m * width * 128 : (m + 1) * width * 128])
    for s in range(3):
        for c in range(6):
            rows = slice((s * 6 + c) * 8, (s * 6 + c) * 8 + 8)
            for r in range(0, width, 2):
                x = jnp.concatenate(
                    [o[rows, r * 128 : r * 128 + 128], o[rows, r * 128 + 128 : r * 128 + 256]], axis=0
                )
                h, l = split(x)
                at = c * 128 + (m * width + r) * 8
                mixed[at : at + 16, s * 128 : s * 128 + 128] = h
                mixed[at : at + 16, 384 + s * 128 : 384 + s * 128 + 128] = l


def far_first(side, inner):
    steps = [
        (x, y, z, core)
        for x in range(side)
        for y in range(side)
        for z in range(side)
        for core in range(inner)
        if x + y + z + core
    ]
    mixed = [steps[(i * 45) % len(steps)] for i in range(len(steps))]
    return sorted(mixed, key=lambda s: -sum(min(k, side - k) for k in s[:3]))


def spline(v):
    m = jnp.abs(v)
    far = jnp.maximum(1.5 - m, 0.0)
    return jnp.where(m < 0.5, 0.75 - m * m, 0.5 * far * far)


def iota(shape, axis):
    return lax.broadcasted_iota(jnp.int32, shape, axis)


def main_kernel(
    devs, side, inner, device_hbm, detail_hbm, penalty_hbm, angles_hbm, field_hbm, tables_hbm, coup_hbm, ov, force,
    uv, tv, cv, u0, u1, t0, t1, r0, r1, p0, p1, w0, w1, k0, k1, pk0, pk1, select, high_mask, low_mask, diag, cb0, cb1,
    device, detail, penalty, angles, comb, ccat, acat, picker, picker_t, taker, taker_t, wts, idx, sbuf, rbuf, bbuf, fbuf,
    in_sem, send_sem, recv_sem, self_sem,
):
    n = uv.shape[0]
    me = lax.axis_index(("chip", "cores"))

    chip_me, core_me = me // inner, me % inner
    my_x, my_y = chip_me // (side * side), chip_me // side % side
    my_zs = [lax.rem(chip_me + k, side) for k in range(side)]
    my_ys = [lax.rem(my_y + k, side) * side for k in range(side)]
    my_xs = [lax.rem(my_x + k, side) * side * side for k in range(side)]
    my_cores = [lax.rem(core_me + k, inner) for k in range(inner)]
    order_z = [side // 2] + [k for k in range(side) if k != side // 2][::-1]

    def for_others(action):
        def line(i, carry):
            y = lax.rem(i // side + side // 2, side)
            x = lax.rem(i + y, side)
            base = (lax.rem(my_x + x, side) * side + lax.rem(my_y + y, side)) * side
            for k in order_z:
                for core in range(inner):
                    who = (base + my_zs[k], my_cores[core])
                    if k == 0 and core == 0:
                        pl.when((x > 0) | (y > 0))(functools.partial(action, who))
                    else:
                        action(who)
            return carry

        lax.fori_loop(0, side * side, line, 0)

    barrier = pltpu.get_barrier_semaphore()
    for_others(
        lambda who: pl.semaphore_signal(barrier, inc=1, device_id=who, device_id_type=MESH)
    )

    groups = 4
    per = n // groups
    loads_u = [
        pltpu.make_async_copy(
            field_hbm.at[pl.ds(g * per, per)], uv.at[pl.ds(g * per, per)], in_sem.at[g]
        )
        for g in range(groups)
    ]
    loads_t = [
        pltpu.make_async_copy(
            tables_hbm.at[pl.ds(g * per, per)], tv.at[pl.ds(g * per, per)], in_sem.at[groups + g]
        )
        for g in range(groups)
    ]
    small = [
        pltpu.make_async_copy(src, dst, in_sem.at[2 * groups + i])
        for i, (src, dst) in enumerate(
            ((device_hbm, device), (detail_hbm, detail), (penalty_hbm, penalty), (angles_hbm, angles), (coup_hbm, cv))
        )
    ]
    for copy in small[0:2] + loads_u + small[2:] + loads_t:
        copy.start()

    small[0].wait()
    small[1].wait()
    lane = iota((128, 128), 1)
    sub = iota((128, 128), 0)
    lane_f = lane.astype(F32)
    sub_f = sub.astype(F32)
    eye = lane == sub
    hit = device[...] == me
    rid = (detail[:, 1, :] * n + detail[:, 0, :]).astype(F32)
    first = jnp.min(jnp.where(hit, lane_f, 1e6), axis=1, keepdims=True)
    last = jnp.max(jnp.where(hit, lane_f, -1.0), axis=1, keepdims=True)
    row0 = jnp.sum(jnp.where(lane_f == first, rid, 0.0), axis=1, keepdims=True)
    row1 = jnp.sum(jnp.where(lane_f == last, rid, 0.0), axis=1, keepdims=True)
    row0 = jnp.where(last >= 0.0, row0, -1.0)
    row1 = jnp.where(last > first, row1, -1.0)

    def to_row(col):
        return jnp.sum(jnp.where(eye, col, 0.0), axis=0, keepdims=True)

    def one_hot(mask):
        return jnp.where(mask, 1.0, 0.0).astype(BF)

    edge_lane = (lane & 63).astype(F32)
    edge_sub = iota((64, 128), 0).astype(F32)
    for k, row in enumerate((row0, row1)):
        picker[k * 128 : k * 128 + 128, :] = one_hot(row == edge_lane)
        flat = one_hot(to_row(row) == edge_sub)
        picker_t[:, k * 256 : k * 256 + 128] = flat
        picker_t[:, k * 256 + 128 : k * 256 + 256] = flat

    dev_row = device[pl.ds(me, 1), :].astype(F32)
    ln_row = detail[me, 3:4, :].astype(F32)
    st_row = detail[me, 2:3, :].astype(F32)
    order = jnp.where(sub < 64, 2 * sub, 2 * sub - 127)
    perm = lane == order

    def to_col(row):
        return jnp.sum(jnp.where(perm, row, 0.0), axis=1, keepdims=True)

    dev_col, ln, st = to_col(dev_row), to_col(ln_row), to_col(st_row)
    slot = jnp.sum(
        jnp.where((dev_row == dev_col) & (lane < order), 1.0, 0.0), axis=1, keepdims=True
    )
    dev_flat, slot_flat = to_row(dev_col), to_row(slot)
    for k in range(2):
        t = one_hot((lane_f == dev_col) & (slot == float(k)))
        taker[:, k * 256 : k * 256 + 128] = t
        taker[:, k * 256 + 128 : k * 256 + 256] = t
        t = one_hot((sub_f == dev_flat) & (slot_flat == float(k)))
        taker_t[k * 128 : k * 128 + 128, 0:128] = t
        taker_t[k * 128 : k * 128 + 128, 128:256] = t

    def strips(p, carry):
        cols = None
        for c in range(6):
            x = uv[p, c]
            comb[p, c : c + 1, :] = 1.5 * x[0:1] - 0.5 * x[1:2]
            comb[n + p, c : c + 1, :] = 1.5 * x[127:128] - 0.5 * x[126:127]
            x = pltpu.roll(x, 2 + 4 * c, 1)
            cols = x if cols is None else jnp.where(lane < 4 * c, cols, x)
        y = jnp.transpose(cols[:, 0:24])
        for c in range(6):
            y0, y1, y2, y3 = (y[4 * c + k : 4 * c + k + 1] for k in range(4))
            comb[2 * n + p, c : c + 1, :] = 1.5 * y2 - 0.5 * y3
            comb[3 * n + p, c : c + 1, :] = 1.5 * y1 - 0.5 * y0
        return carry

    def strips_pair(i, carry):
        return strips(2 * i + 1, strips(2 * i, carry))

    for g in range(groups):
        loads_u[g].wait()
        lax.fori_loop(g * per // 2, (g + 1) * per // 2, strips_pair, 0)
    for c in range(6):
        h, l = split(comb[:, c, :])
        ccat[0:64, c * 128 : c * 128 + 128] = h
        ccat[64:128, c * 128 : c * 128 + 128] = l
    for k in range(2):
        slots = dot(picker[k * 128 : k * 128 + 128, :], ccat[...])
        for c in range(6):
            sbuf[k * 6 + c] = slots[:, c * 128 : c * 128 + 128]
    unit = st * 256.0 + (2.0 * lane_f + 1.0) * ln
    near = jnp.floor((unit + 128.0) * (1.0 / 256.0))
    for tap in range(3):
        j = near + float(tap - 1)
        w = spline(unit * (1.0 / 256.0) - j)
        wts[tap] = jnp.where((j >= 0.0) & (j <= 127.0), w, 0.0)
        idx[tap] = jnp.clip(j, 0.0, 127.0).astype(jnp.int32)
    low = jnp.floor(((256.0 * (lane_f - st) - 384.0) / ln - 1.0) * 0.5) + 1.0
    for tap in range(6):
        q = low + float(tap)
        v = (st * 256.0 + (2.0 * q + 1.0) * ln) * (1.0 / 256.0) - lane_f
        wts[3 + tap] = jnp.where((q >= 0.0) & (q <= 127.0), spline(v), 0.0)
        idx[3 + tap] = jnp.clip(q, 0.0, 127.0).astype(jnp.int32)

    consts = (select, high_mask, low_mask, diag)
    kron_constants(*consts)
    pl.semaphore_wait(barrier, devs - 1)

    def exchange(src, dst, which):
        def send(who):
            pltpu.make_async_remote_copy(
                src_ref=src.at[:, who[0] * inner + who[1], :],
                dst_ref=dst.at[:, me, :],
                send_sem=send_sem.at[which],
                recv_sem=recv_sem.at[which],
                device_id=who,
                device_id_type=MESH,
            ).start()

        for x, y, z, core in far_first(side, inner):
            send((my_xs[x] + my_ys[y] + my_zs[z], my_cores[core]))
        pltpu.make_async_copy(src.at[:, me, :], dst.at[:, me, :], self_sem.at[which]).start()

    def settle(src, dst, which):
        others = pl.ds(0, devs - 1)
        for sem in (send_sem, recv_sem):
            pltpu.make_async_copy(src.at[:, others, :], dst.at[:, others, :], sem.at[which]).wait()
        pltpu.make_async_copy(src.at[:, me, :], dst.at[:, me, :], self_sem.at[which]).wait()

    exchange(sbuf, rbuf, 0)

    bufs = ((u0, t0, r0, p0, w0, k0, pk0, cb0), (u1, t1, r1, p1, w1, k1, pk1, cb1))
    small[4].wait()
    prep_coupling(cv, 0, cb0)
    prep_coupling(cv, 1, cb1)
    for copy in loads_t:
        copy.wait()

    def stage(p, j):
        u, t, r, pr, w, kr, pk, cb = bufs[j]
        un, tn, rn, prn, wn, krn, pkn, cbn = bufs[1 - j]
        before = jnp.maximum(p - 1, 0)
        later = jnp.minimum(p + 2, n - 1)
        seqs = (
            [
                lambda: left_products(tn, un, prn, 0),
                lambda: left_products(tn, un, prn, 1),
                lambda: stack(prn, pkn, 0),
                lambda: left_products(tn, un, prn, 2),
                lambda: stack(prn, pkn, 1),
            ]
            + [lambda: mix(kr, pk, w, 0, WIDTH), lambda: stack(prn, pkn, 2)]
            + [lambda k=k: mix(kr, pk, w, k, WIDTH) for k in range(1, 16 // WIDTH)]
            + [
                lambda: right_products(wn, rn, ov.at[before]),
                lambda: make_kron(cbn, *consts, krn),
            ],
            [lambda: prep_coupling(cv, later, cb)]
            + [lambda c=c: prep_field(uv.at[later], u, c) for c in range(6)]
            + [lambda k=k: prep_left(tv.at[later], t, k) for k in range(3)]
            + [lambda k=k: prep_right(tv.at[p], r, k) for k in range(3)],
        )
        keyed = [((i + 0.5) / len(q), f) for q in seqs for i, f in enumerate(q)]
        for _, f in sorted(keyed, key=lambda z: z[0]):
            f()

    def pair(h, carry):
        stage(2 * h, 0)
        stage(2 * h + 1, 1)
        return carry

    for i in range(2):
        for c in range(6):
            prep_field(uv.at[i], bufs[i][0], c)
        for k in range(3):
            prep_left(tv.at[i], bufs[i][1], k)
    for m in range(3):
        left_products(t0, u0, p0, m)
        stack(p0, pk0, m)
    make_kron(cb0, *consts, k0)
    half = n // 4
    lax.fori_loop(0, half, pair, 0)

    settle(sbuf, rbuf, 0)

    def slots_of(buf):
        for k in range(2):
            for c in range(6):
                h, l = split(buf[k * 6 + c])
                cols = slice(c * 128, c * 128 + 128)
                acat[k * 256 : k * 256 + 128, cols] = h
                acat[k * 256 + 128 : k * 256 + 256, cols] = l

    slots_of(rbuf)
    strip = dot(taker[...], acat[...])

    def taps(x, start, count, rows):
        total = None
        for tap in range(start, start + count):
            v = jnp.take_along_axis(x, idx[tap, rows, :], axis=1) * wts[tap, rows, :]
            total = v if total is None else total + v
        return total

    own = n * 4
    first_rows, second_rows = slice(0, own), slice(own, 2 * own)
    tr_a, tr_b = [], []
    for c in range(6):
        cols = slice(c * 128, c * 128 + 128)
        tr_a.append(taps(strip[0:own, cols], 0, 3, first_rows))
        tr_b.append(taps(strip[own : 2 * own, cols], 0, 3, second_rows))
    small[2].wait()
    small[3].wait()
    half_eye = iota((own, own), 0) == iota((own, own), 1)
    ang = jnp.concatenate(
        [
            jnp.sum(jnp.where(half_eye, angles[k : k + 1, :], 0.0), axis=1, keepdims=True)
            for k in range(3)
        ],
        axis=1,
    )
    cosv, sinv = jnp.cos(ang), jnp.sin(ang)
    ca, cb_, cg = (cosv[:, k : k + 1] for k in range(3))
    sa, sb, sg = (sinv[:, k : k + 1] for k in range(3))
    rot = (
        (cg * cb_, cg * sb * sa - sg * ca, cg * sb * ca + sg * sa),
        (sg * cb_, sg * sb * sa + cg * ca, sg * sb * ca - cg * sa),
        (-sb, cb_ * sa, cb_ * ca),
    )
    for blk in range(2):
        pen = penalty[:, blk, :]
        load = []
        for c in range(3):
            turned = sum(rot[c][d] * tr_b[3 * blk + d] for d in range(3))
            load.append(pen * (tr_a[3 * blk + c] - turned))
        for c in range(3):
            back = -sum(rot[d][c] * load[d] for d in range(3))
            cols = slice((3 * blk + c) * 128, (3 * blk + c) * 128 + 128)
            for x, rows in ((load[c], first_rows), (back, second_rows)):
                h, l = split(taps(x, 3, 6, rows))
                acat[rows, cols] = h
                acat[128 + rows.start : 128 + rows.stop, cols] = l
    for k in range(2):
        slots = dot(taker_t[k * 128 : k * 128 + 128, :], acat[0:256, :])
        for c in range(6):
            bbuf[k * 6 + c] = slots[:, c * 128 : c * 128 + 128]
    exchange(bbuf, fbuf, 1)

    lax.fori_loop(half, n // 2, pair, 0)
    right_products(w1, r1, ov.at[n - 1])

    settle(bbuf, fbuf, 1)
    slots_of(fbuf)
    gathered = dot(picker_t[...], acat[...])
    for c in range(6):
        force[:, c, :] = gathered[:, c * 128 : c * 128 + 128]


def add_kernel(part, force, out_hbm, buf, out_sem):
    n = buf.shape[0]

    def put(p):
        return pltpu.make_async_copy(buf.at[p], out_hbm.at[p], out_sem)

    lane = iota((8, 128), 1)
    sub = iota((8, 128), 0)
    left = jnp.where(lane == 0, 1.5, jnp.where(lane == 1, -0.5, 0.0))
    right = jnp.where(lane == 127, 1.5, jnp.where(lane == 126, -0.5, 0.0))
    spread = jnp.where(sub < 2, left, jnp.where(sub < 4, right, 0.0)).astype(BF)
    top = jnp.where(sub == 0, 1.5, jnp.where(sub == 1, -0.5, 0.0))
    bottom = jnp.where(sub == 7, 1.5, jnp.where(sub == 6, -0.5, 0.0))

    def one(p, carry):
        for c in range(6):
            f0 = force[p, c : c + 1, :]
            f1 = force[n + p, c : c + 1, :]
            f2 = force[2 * n + p, c : c + 1, :]
            f3 = force[3 * n + p, c : c + 1, :]
            h2, l2 = f2.astype(BF).astype(F32), f2 - f2.astype(BF).astype(F32)
            h3, l3 = f3.astype(BF).astype(F32), f3 - f3.astype(BF).astype(F32)
            rows = jnp.where(
                sub == 0, h2, jnp.where(sub == 1, l2, jnp.where(sub == 2, h3, jnp.where(sub == 3, l3, 0.0)))
            ).astype(BF)
            cells = lax.dot_general(
                rows, spread, (((0,), (0,)), ((), ())), preferred_element_type=F32
            )
            buf[p, c] = part[p, c] + cells
            buf[p, c, 0:8, :] = buf[p, c, 0:8, :] + top * f0
            buf[p, c, 120:128, :] = buf[p, c, 120:128, :] + bottom * f1
        put(p).start()
        return carry

    lax.fori_loop(0, n // 2, lambda i, carry: one(2 * i + 1, one(2 * i, carry)), 0)
    pltpu.make_async_copy(buf, out_hbm, out_sem).wait()


def shards(devs, side, inner, patch_field, patch_tables, coupling, side_device, side_detail, penalty, angles):
    n = patch_field.shape[0]
    detail = side_detail.reshape(devs, 128, 4).transpose(0, 2, 1)
    device = side_device.reshape(devs, 128)
    coup = coupling.transpose(1, 2, 3, 0)
    pin = functools.partial(pltpu.with_memory_space_constraint, memory_space=pltpu.HBM)
    device, detail, coup, penalty, angles_t = pin(device), pin(detail), pin(coup), pin(penalty), pin(angles.T)
    anyspec = pl.BlockSpec(memory_space=pltpu.HBM)
    vspec = pl.BlockSpec(memory_space=pltpu.VMEM)
    v = pltpu.VMEM
    big = v(patch_field.shape, F32)
    wire = v((12, devs, 128), F32)
    dma = pltpu.SemaphoreType.DMA
    part, force = pl.pallas_call(
        functools.partial(main_kernel, devs, side, inner),
        out_shape=(
            jax.ShapeDtypeStruct(patch_field.shape, F32),
            jax.ShapeDtypeStruct((4 * n, 6, 128), F32),
        ),
        in_specs=[anyspec] * 7,
        out_specs=(vspec, vspec),
        scratch_shapes=[big, big, v(coup.shape, F32)]
        + [v((384, 768), BF)] * 2
        + [v((384, 384), BF)] * 2
        + [v((256, 384), BF)] * 2
        + [v((384, 768), F32)] * 2
        + [v((768, 768), BF)] * 2
        + [v((144, 432), BF)] * 2
        + [
            v((432, 2048), BF),
            v((432, 2048), BF),
            v((144, 240), BF),
            v((240, 432), BF),
            v((240, 432), BF),
            v((144, 432), F32),
            v((240, 128), F32),
            v((240, 128), F32),
            v((devs, 128), jnp.int32),
            v((devs, 4, 128), jnp.int32),
            v(penalty.shape, F32),
            v((3, penalty.shape[0]), F32),
            v((64, 6, 128), F32),
            v((128, 768), BF),
            v((512, 768), BF),
            v((256, 128), BF),
            v((64, 512), BF),
            v((128, 512), BF),
            v((256, 256), BF),
            v((9, 128, 128), F32),
            v((9, 128, 128), jnp.int32),
        ]
        + [wire] * 4
        + [dma((13,)), dma((2,)), dma((2,)), dma((2,))],
        compiler_params=pltpu.CompilerParams(
            collective_id=0, has_side_effects=True, vmem_limit_bytes=47 * 2**20
        ),
    )(device, detail, penalty, angles_t, patch_field, patch_tables, coup)
    return pl.pallas_call(
        add_kernel,
        out_shape=jax.ShapeDtypeStruct(patch_field.shape, F32),
        in_specs=[vspec, vspec],
        out_specs=anyspec,
        scratch_shapes=[big, dma],
        compiler_params=pltpu.CompilerParams(vmem_limit_bytes=16 * 2**20),
    )(part, force)


def solution(mesh):
    devs = mesh.shape["chip"] * mesh.shape["cores"]
    return jax.shard_map(
        functools.partial(shards, devs, round(mesh.shape["chip"] ** (1 / 3)), mesh.shape["cores"]),
        mesh=mesh,
        in_specs=(
            P(("chip", "cores"), None, None, None),
            P(("chip", "cores"), None, None, None),
            P(("chip", "cores"), None, None, None),
            P(),
            P(),
            P(("chip", "cores"), None, None),
            P(("chip", "cores"), None),
        ),
        out_specs=P(("chip", "cores"), None, None, None),
        check_vma=False,
    )
```

```python
import functools

import jax
import jax.numpy as jnp
from jax import lax
from jax.experimental import pallas as pl
from jax.experimental.pallas import tpu as pltpu
from jax.sharding import PartitionSpec as P

BF = jnp.bfloat16
F32 = jnp.float32
MESH = pl.DeviceIdType.MESH
WIDTH = 4


def split(x):
    high = x.astype(BF)
    return high, (x - high.astype(F32)).astype(BF)


def dot(a, b):
    return lax.dot_general(a, b, (((1,), (0,)), ((), ())), preferred_element_type=F32)


def dot_t(a, b):
    return lax.dot_general(a, b, (((1,), (1,)), ((), ())), preferred_element_type=F32)


def prep_field(field, ucat, c):
    h, l = split(field[c])
    cols = slice(c * 128, c * 128 + 128)
    ucat[0:128, cols] = h
    ucat[128:256, cols] = l
    ucat[256:384, cols] = h


def prep_left(tables, tcat, t):
    h, l = split(tables[t])
    rows = slice(t * 128, t * 128 + 128)
    tcat[rows, 0:128] = h
    tcat[rows, 128:256] = h
    tcat[rows, 256:384] = l


def prep_right(tables, rcat, s):
    h, l = split(tables[(4, 3, 5)[s]])
    cols = slice(s * 128, s * 128 + 128)
    rcat[0:128, cols] = h
    rcat[128:256, cols] = l


def prep_coupling(coup, p, cb):
    lane = iota((8, coup.shape[3]), 1)
    for t in range(5):
        for c in range(6):
            tile = jnp.concatenate([coup[t, c], jnp.zeros((2, coup.shape[3]), F32)], axis=0)
            value = jnp.sum(jnp.where(lane == p, tile, 0.0), axis=1, keepdims=True)
            row = (t * 6 + c) * 8
            cb[row : row + 8, :] = jnp.broadcast_to(value, (8, 128))


def left_products(tcat, ucat, prod, m):
    cols = slice(m * 256, m * 256 + 256)
    prod[:, cols] = dot(tcat[...], ucat[:, cols])


def right_products(mixed, rcat, out):
    o = dot_t(mixed[:, 0:384], rcat[...])
    o2 = dot_t(mixed[:, 384:768], rcat[0:128, :])
    for c in range(6):
        q = slice(c * 128, c * 128 + 128)
        out[c] = (o[q, 0:128] + o[q, 128:256]) + o2[q]


def kron_constants(select, high_mask, low_mask, diag):
    row, col = iota(select.shape, 0) // 8, iota(select.shape, 1) // 8
    kind, term = row // 6, col // 6
    used = ((kind == 0) & ((term == 0) | (term >= 3))) | ((kind > 0) & (term == kind))
    select[...] = jnp.where(used & (row % 6 == col % 6), 1.0, 0.0).astype(BF)
    row, col = iota(high_mask.shape, 0), iota(high_mask.shape, 1) // 8
    term, d = row // 48, row % 8
    table = jnp.where(term >= 3, term - 2, term)
    part, block = col // 18, col % 18
    match = (table == block // 6) & (d == block % 6)
    high_mask[...] = jnp.where(match & (part < 2), 1.0, 0.0).astype(BF)
    low_mask[...] = jnp.where(match & (part == 2), 1.0, 0.0).astype(BF)
    row, col = iota(diag.shape, 0), iota(diag.shape, 1)
    diag[...] = jnp.where(row % 8 == col % 8, 1.0, 0.0)


def make_kron(cb, select, high_mask, low_mask, diag, kron):
    h, l = split(cb[...])
    parts = []
    for k in range(0, 432, 128):
        n = min(128, 432 - k)
        cols = slice(k, k + n)
        parts.append(h[:, 0:n] * high_mask[:, cols] + l[:, 0:n] * low_mask[:, cols])
    kron[...] = (dot(select[...], jnp.concatenate(parts, axis=1)) * diag[...]).astype(BF)


def stack_products(prod, pk, m):
    t, d = m // 3, 2 * (m % 3)
    for r in range(16):
        rows = slice(t * 128 + 8 * r, t * 128 + 8 * r + 8)
        x = jnp.concatenate(
            [prod[rows, d * 128 : d * 128 + 128], prod[rows, d * 128 + 128 : d * 128 + 256]], axis=0
        )
        h, l = split(x)
        cols = slice(r * 128, r * 128 + 128)
        pk[16 * m : 16 * m + 16, cols] = h
        pk[144 + 16 * m : 160 + 16 * m, cols] = l
        pk[288 + 16 * m : 304 + 16 * m, cols] = h


def stack(prod, pk, m):
    for t in range(3):
        stack_products(prod, pk, 3 * t + m)


def mix(kron, pk, mixed, m, width):
    o = dot(kron[...], pk[:, m * width * 128 : (m + 1) * width * 128])
    for s in range(3):
        for c in range(6):
            rows = slice((s * 6 + c) * 8, (s * 6 + c) * 8 + 8)
            for r in range(0, width, 2):
                x = jnp.concatenate(
                    [o[rows, r * 128 : r * 128 + 128], o[rows, r * 128 + 128 : r * 128 + 256]], axis=0
                )
                h, l = split(x)
                at = c * 128 + (m * width + r) * 8
                mixed[at : at + 16, s * 128 : s * 128 + 128] = h
                mixed[at : at + 16, 384 + s * 128 : 384 + s * 128 + 128] = l


def far_first(side, inner):
    steps = [
        (x, y, z, core)
        for x in range(side)
        for y in range(side)
        for z in range(side)
        for core in range(inner)
        if x + y + z + core
    ]
    mixed = [steps[(i * 45) % len(steps)] for i in range(len(steps))]
    return sorted(mixed, key=lambda s: -sum(min(k, side - k) for k in s[:3]))


def spline(v):
    m = jnp.abs(v)
    far = jnp.maximum(1.5 - m, 0.0)
    return jnp.where(m < 0.5, 0.75 - m * m, 0.5 * far * far)


def iota(shape, axis):
    return lax.broadcasted_iota(jnp.int32, shape, axis)


def main_kernel(
    devs, side, inner, device_hbm, detail_hbm, penalty_hbm, angles_hbm, field_hbm, tables_hbm, coup_hbm, ov, force,
    uv, tv, cv, u0, u1, t0, t1, r0, r1, p0, p1, w0, w1, k0, k1, pk0, pk1, select, high_mask, low_mask, diag, rot, cb0, cb1,
    device, detail, penalty, angles, comb, ccat, acat, picker, picker_t, taker, taker_t, wts, idx, sbuf, rbuf, bbuf, fbuf,
    in_sem, send_sem, recv_sem, self_sem,
):
    n = uv.shape[0]
    me = lax.axis_index(("chip", "cores"))

    chip_me, core_me = me // inner, me % inner
    my_x, my_y = chip_me // (side * side), chip_me // side % side
    my_zs = [lax.rem(chip_me + k, side) for k in range(side)]
    my_ys = [lax.rem(my_y + k, side) * side for k in range(side)]
    my_xs = [lax.rem(my_x + k, side) * side * side for k in range(side)]
    my_cores = [lax.rem(core_me + k, inner) for k in range(inner)]

    def others():
        for x, y, z, core in far_first(side, inner):
            yield my_xs[x] + my_ys[y] + my_zs[z], my_cores[core]

    barrier = pltpu.get_barrier_semaphore()
    greeted = list(others())

    groups = 4
    per = n // groups
    loads_u = [
        pltpu.make_async_copy(
            field_hbm.at[pl.ds(g * per, per)], uv.at[pl.ds(g * per, per)], in_sem.at[g]
        )
        for g in range(groups)
    ]
    loads_t = [
        pltpu.make_async_copy(
            tables_hbm.at[pl.ds(g * per, per)], tv.at[pl.ds(g * per, per)], in_sem.at[groups + g]
        )
        for g in range(groups)
    ]
    small = [
        pltpu.make_async_copy(src, dst, in_sem.at[2 * groups + i])
        for i, (src, dst) in enumerate(
            ((device_hbm, device), (detail_hbm, detail), (penalty_hbm, penalty), (angles_hbm, angles), (coup_hbm, cv))
        )
    ]
    for copy in small[0:2] + loads_u + small[2:] + loads_t:
        copy.start()

    for who in greeted:
        pl.semaphore_signal(barrier, inc=1, device_id=who, device_id_type=MESH)

    small[0].wait()
    small[1].wait()
    lane = iota((128, 128), 1)
    sub = iota((128, 128), 0)
    lane_f = lane.astype(F32)
    sub_f = sub.astype(F32)
    eye = lane == sub
    hit = device[...] == me
    rid = (detail[:, 1, :] * n + detail[:, 0, :]).astype(F32)
    first = jnp.min(jnp.where(hit, lane_f, 1e6), axis=1, keepdims=True)
    last = jnp.max(jnp.where(hit, lane_f, -1.0), axis=1, keepdims=True)
    row0 = jnp.sum(jnp.where(lane_f == first, rid, 0.0), axis=1, keepdims=True)
    row1 = jnp.sum(jnp.where(lane_f == last, rid, 0.0), axis=1, keepdims=True)
    row0 = jnp.where(last >= 0.0, row0, -1.0)
    row1 = jnp.where(last > first, row1, -1.0)

    def to_row(col):
        return jnp.sum(jnp.where(eye, col, 0.0), axis=0, keepdims=True)

    def one_hot(mask):
        return jnp.where(mask, 1.0, 0.0).astype(BF)

    edge_lane = (lane & 63).astype(F32)
    edge_sub = iota((64, 128), 0).astype(F32)
    for k, row in enumerate((row0, row1)):
        picker[k * 128 : k * 128 + 128, :] = one_hot(row == edge_lane)
        flat = one_hot(to_row(row) == edge_sub)
        picker_t[:, k * 256 : k * 256 + 128] = flat
        picker_t[:, k * 256 + 128 : k * 256 + 256] = flat

    dev_row = device[pl.ds(me, 1), :].astype(F32)
    ln_row = detail[me, 3:4, :].astype(F32)
    st_row = detail[me, 2:3, :].astype(F32)
    order = jnp.where(sub < 64, 2 * sub, 2 * sub - 127)
    perm = lane == order

    def to_col(row):
        return jnp.sum(jnp.where(perm, row, 0.0), axis=1, keepdims=True)

    dev_col, ln, st = to_col(dev_row), to_col(ln_row), to_col(st_row)
    slot = jnp.sum(
        jnp.where((dev_row == dev_col) & (lane < order), 1.0, 0.0), axis=1, keepdims=True
    )
    dev_flat, slot_flat = to_row(dev_col), to_row(slot)
    for k in range(2):
        t = one_hot((lane_f == dev_col) & (slot == float(k)))
        taker[:, k * 256 : k * 256 + 128] = t
        taker[:, k * 256 + 128 : k * 256 + 256] = t
        t = one_hot((sub_f == dev_flat) & (slot_flat == float(k)))
        taker_t[k * 128 : k * 128 + 128, 0:128] = t
        taker_t[k * 128 : k * 128 + 128, 128:256] = t

    def strips(p, carry):
        cols = None
        for c in range(6):
            x = uv[p, c]
            comb[p, c : c + 1, :] = 1.5 * x[0:1] - 0.5 * x[1:2]
            comb[n + p, c : c + 1, :] = 1.5 * x[127:128] - 0.5 * x[126:127]
            x = pltpu.roll(x, 2 + 4 * c, 1)
            cols = x if cols is None else jnp.where(lane < 4 * c, cols, x)
        y = jnp.transpose(cols[:, 0:24])
        for c in range(6):
            y0, y1, y2, y3 = (y[4 * c + k : 4 * c + k + 1] for k in range(4))
            comb[2 * n + p, c : c + 1, :] = 1.5 * y2 - 0.5 * y3
            comb[3 * n + p, c : c + 1, :] = 1.5 * y1 - 0.5 * y0
        return carry

    def strips_pair(i, carry):
        return strips(2 * i + 1, strips(2 * i, carry))

    for g in range(groups):
        loads_u[g].wait()
        lax.fori_loop(g * per // 2, (g + 1) * per // 2, strips_pair, 0)
    for c in range(6):
        h, l = split(comb[:, c, :])
        ccat[0:64, c * 128 : c * 128 + 128] = h
        ccat[64:128, c * 128 : c * 128 + 128] = l
    for k in range(2):
        slots = dot(picker[k * 128 : k * 128 + 128, :], ccat[...])
        for c in range(6):
            sbuf[k * 6 + c] = slots[:, c * 128 : c * 128 + 128]
    unit = st * 256.0 + (2.0 * lane_f + 1.0) * ln
    near = jnp.floor((unit + 128.0) * (1.0 / 256.0))
    for tap in range(3):
        j = near + float(tap - 1)
        w = spline(unit * (1.0 / 256.0) - j)
        wts[tap] = jnp.where((j >= 0.0) & (j <= 127.0), w, 0.0)
        idx[tap] = jnp.clip(j, 0.0, 127.0).astype(jnp.int32)
    low = jnp.floor(((256.0 * (lane_f - st) - 384.0) / ln - 1.0) * 0.5) + 1.0
    for tap in range(6):
        q = low + float(tap)
        v = (st * 256.0 + (2.0 * q + 1.0) * ln) * (1.0 / 256.0) - lane_f
        wts[3 + tap] = jnp.where((q >= 0.0) & (q <= 127.0), spline(v), 0.0)
        idx[3 + tap] = jnp.clip(q, 0.0, 127.0).astype(jnp.int32)

    consts = (select, high_mask, low_mask, diag)
    kron_constants(*consts)
    small[3].wait()
    own = n * 4
    half_eye = iota((own, own), 0) == iota((own, own), 1)
    ang = jnp.concatenate(
        [
            jnp.sum(jnp.where(half_eye, angles[k : k + 1, :], 0.0), axis=1, keepdims=True)
            for k in range(3)
        ],
        axis=1,
    )
    cosv, sinv = jnp.cos(ang), jnp.sin(ang)
    ca, cb_, cg = (cosv[:, k : k + 1] for k in range(3))
    sa, sb, sg = (sinv[:, k : k + 1] for k in range(3))
    entries = (
        (cg * cb_, cg * sb * sa - sg * ca, cg * sb * ca + sg * sa),
        (sg * cb_, sg * sb * sa + cg * ca, sg * sb * ca - cg * sa),
        (-sb, cb_ * sa, cb_ * ca),
    )
    for k in range(9):
        rot[k] = jnp.broadcast_to(entries[k // 3][k % 3], (own, 128))
    pl.semaphore_wait(barrier, devs - 1)

    def exchange(src, dst, which):
        def send(who):
            pltpu.make_async_remote_copy(
                src_ref=src.at[:, who[0] * inner + who[1], :],
                dst_ref=dst.at[:, me, :],
                send_sem=send_sem.at[which],
                recv_sem=recv_sem.at[which],
                device_id=who,
                device_id_type=MESH,
            ).start()

        for who in others():
            send(who)
        pltpu.make_async_copy(src.at[:, me, :], dst.at[:, me, :], self_sem.at[which]).start()

    def settle(src, dst, which):
        others = pl.ds(0, devs - 1)
        for sem in (send_sem, recv_sem):
            pltpu.make_async_copy(src.at[:, others, :], dst.at[:, others, :], sem.at[which]).wait()
        pltpu.make_async_copy(src.at[:, me, :], dst.at[:, me, :], self_sem.at[which]).wait()

    exchange(sbuf, rbuf, 0)

    bufs = ((u0, t0, r0, p0, w0, k0, pk0, cb0), (u1, t1, r1, p1, w1, k1, pk1, cb1))
    small[4].wait()
    prep_coupling(cv, 0, cb0)
    prep_coupling(cv, 1, cb1)
    for copy in loads_t:
        copy.wait()

    def stage(p, j):
        u, t, r, pr, w, kr, pk, cb = bufs[j]
        un, tn, rn, prn, wn, krn, pkn, cbn = bufs[1 - j]
        before = jnp.maximum(p - 1, 0)
        later = jnp.minimum(p + 2, n - 1)
        seqs = (
            [
                lambda: left_products(tn, un, prn, 0),
                lambda: left_products(tn, un, prn, 1),
                lambda: stack(prn, pkn, 0),
                lambda: left_products(tn, un, prn, 2),
                lambda: stack(prn, pkn, 1),
            ]
            + [lambda: mix(kr, pk, w, 0, WIDTH), lambda: stack(prn, pkn, 2)]
            + [lambda k=k: mix(kr, pk, w, k, WIDTH) for k in range(1, 16 // WIDTH)]
            + [
                lambda: right_products(wn, rn, ov.at[before]),
                lambda: make_kron(cbn, *consts, krn),
            ],
            [lambda: prep_coupling(cv, later, cb)]
            + [lambda c=c: prep_field(uv.at[later], u, c) for c in range(6)]
            + [lambda k=k: prep_left(tv.at[later], t, k) for k in range(3)]
            + [lambda k=k: prep_right(tv.at[p], r, k) for k in range(3)],
        )
        keyed = [((i + 0.5) / len(q), f) for q in seqs for i, f in enumerate(q)]
        for _, f in sorted(keyed, key=lambda z: z[0]):
            f()

    def pair(h, carry):
        stage(2 * h, 0)
        stage(2 * h + 1, 1)
        return carry

    for i in range(2):
        for c in range(6):
            prep_field(uv.at[i], bufs[i][0], c)
        for k in range(3):
            prep_left(tv.at[i], bufs[i][1], k)
    for m in range(3):
        left_products(t0, u0, p0, m)
        stack(p0, pk0, m)
    make_kron(cb0, *consts, k0)
    half = n // 4
    lax.fori_loop(0, half, pair, 0)

    settle(sbuf, rbuf, 0)

    def slots_of(buf):
        for k in range(2):
            for c in range(6):
                h, l = split(buf[k * 6 + c])
                cols = slice(c * 128, c * 128 + 128)
                acat[k * 256 : k * 256 + 128, cols] = h
                acat[k * 256 + 128 : k * 256 + 256, cols] = l

    slots_of(rbuf)
    strip = dot(taker[...], acat[...])

    def taps(xs, start, count, row):
        totals = [None] * 6
        rows = slice(row, row + 8)
        for tap in range(start, start + count):
            where, weight = idx[tap, rows, :], wts[tap, rows, :]
            for c in range(6):
                v = jnp.take_along_axis(xs[c], where, axis=1) * weight
                totals[c] = v if totals[c] is None else totals[c] + v
        return totals

    def turn(row, entries, values):
        parts = [rot[e, row : row + 8, :] * v for e, v in zip(entries, values)]
        return parts[0] + parts[1] + parts[2]

    small[2].wait()
    for at in range(0, own, 16):
        halves = []
        for row in (at, at + 8):
            near_t, far_t = (
                taps([strip[r : r + 8, c * 128 : c * 128 + 128] for c in range(6)], 0, 3, r)
                for r in (row, own + row)
            )
            near_l, far_l = [], []
            for blk in (0, 3):
                weight = penalty[row : row + 8, blk // 3, :]
                for c in range(3):
                    turned = turn(row, (3 * c, 3 * c + 1, 3 * c + 2), far_t[blk : blk + 3])
                    near_l.append(weight * (near_t[blk + c] - turned))
                for c in range(3):
                    far_l.append(-turn(row, (c, 3 + c, 6 + c), near_l[blk : blk + 3]))
            halves.append((taps(near_l, 3, 6, row), taps(far_l, 3, 6, own + row)))
        for which in range(2):
            base = which * own + at
            for c in range(6):
                h, l = split(jnp.concatenate([halves[0][which][c], halves[1][which][c]], axis=0))
                cols = slice(c * 128, c * 128 + 128)
                acat[base : base + 16, cols] = h
                acat[128 + base : 144 + base, cols] = l
    for k in range(2):
        slots = dot(taker_t[k * 128 : k * 128 + 128, :], acat[0:256, :])
        for c in range(6):
            bbuf[k * 6 + c] = slots[:, c * 128 : c * 128 + 128]
    exchange(bbuf, fbuf, 1)

    lax.fori_loop(half, n // 2, pair, 0)
    right_products(w1, r1, ov.at[n - 1])

    settle(bbuf, fbuf, 1)
    slots_of(fbuf)
    gathered = dot(picker_t[...], acat[...])
    for c in range(6):
        force[:, c, :] = gathered[:, c * 128 : c * 128 + 128]


def add_kernel(part, force, out_hbm, buf, out_sem):
    n = buf.shape[0]

    def put(p):
        return pltpu.make_async_copy(buf.at[p], out_hbm.at[p], out_sem)

    lane = iota((8, 128), 1)
    sub = iota((8, 128), 0)
    left = jnp.where(lane == 0, 1.5, jnp.where(lane == 1, -0.5, 0.0))
    right = jnp.where(lane == 127, 1.5, jnp.where(lane == 126, -0.5, 0.0))
    spread = jnp.where(sub < 2, left, jnp.where(sub < 4, right, 0.0)).astype(BF)
    top = jnp.where(sub == 0, 1.5, jnp.where(sub == 1, -0.5, 0.0))
    bottom = jnp.where(sub == 7, 1.5, jnp.where(sub == 6, -0.5, 0.0))

    def one(p, carry):
        for c in range(6):
            f0 = force[p, c : c + 1, :]
            f1 = force[n + p, c : c + 1, :]
            f2 = force[2 * n + p, c : c + 1, :]
            f3 = force[3 * n + p, c : c + 1, :]
            h2, l2 = f2.astype(BF).astype(F32), f2 - f2.astype(BF).astype(F32)
            h3, l3 = f3.astype(BF).astype(F32), f3 - f3.astype(BF).astype(F32)
            rows = jnp.where(
                sub == 0, h2, jnp.where(sub == 1, l2, jnp.where(sub == 2, h3, jnp.where(sub == 3, l3, 0.0)))
            ).astype(BF)
            cells = lax.dot_general(
                rows, spread, (((0,), (0,)), ((), ())), preferred_element_type=F32
            )
            buf[p, c] = part[p, c] + cells
            buf[p, c, 0:8, :] = buf[p, c, 0:8, :] + top * f0
            buf[p, c, 120:128, :] = buf[p, c, 120:128, :] + bottom * f1
        put(p).start()
        return carry

    lax.fori_loop(0, n // 2, lambda i, carry: one(2 * i + 1, one(2 * i, carry)), 0)
    pltpu.make_async_copy(buf, out_hbm, out_sem).wait()


def shards(devs, side, inner, patch_field, patch_tables, coupling, side_device, side_detail, penalty, angles):
    n = patch_field.shape[0]
    detail = side_detail.reshape(devs, 128, 4).transpose(0, 2, 1)
    device = side_device.reshape(devs, 128)
    coup = coupling.transpose(1, 2, 3, 0)
    pin = functools.partial(pltpu.with_memory_space_constraint, memory_space=pltpu.HBM)
    device, detail, coup, penalty, angles_t = pin(device), pin(detail), pin(coup), pin(penalty), pin(angles.T)
    anyspec = pl.BlockSpec(memory_space=pltpu.HBM)
    vspec = pl.BlockSpec(memory_space=pltpu.VMEM)
    v = pltpu.VMEM
    big = v(patch_field.shape, F32)
    wire = v((12, devs, 128), F32)
    dma = pltpu.SemaphoreType.DMA
    part, force = pl.pallas_call(
        functools.partial(main_kernel, devs, side, inner),
        out_shape=(
            jax.ShapeDtypeStruct(patch_field.shape, F32),
            jax.ShapeDtypeStruct((4 * n, 6, 128), F32),
        ),
        in_specs=[anyspec] * 7,
        out_specs=(vspec, vspec),
        scratch_shapes=[big, big, v(coup.shape, F32)]
        + [v((384, 768), BF)] * 2
        + [v((384, 384), BF)] * 2
        + [v((256, 384), BF)] * 2
        + [v((384, 768), F32)] * 2
        + [v((768, 768), BF)] * 2
        + [v((144, 432), BF)] * 2
        + [
            v((432, 2048), BF),
            v((432, 2048), BF),
            v((144, 240), BF),
            v((240, 432), BF),
            v((240, 432), BF),
            v((144, 432), F32),
            v((9, penalty.shape[0], 128), F32),
            v((240, 128), F32),
            v((240, 128), F32),
            v((devs, 128), jnp.int32),
            v((devs, 4, 128), jnp.int32),
            v(penalty.shape, F32),
            v((3, penalty.shape[0]), F32),
            v((64, 6, 128), F32),
            v((128, 768), BF),
            v((512, 768), BF),
            v((256, 128), BF),
            v((64, 512), BF),
            v((128, 512), BF),
            v((256, 256), BF),
            v((9, 128, 128), F32),
            v((9, 128, 128), jnp.int32),
        ]
        + [wire] * 4
        + [dma((13,)), dma((2,)), dma((2,)), dma((2,))],
        compiler_params=pltpu.CompilerParams(
            collective_id=0, has_side_effects=True, vmem_limit_bytes=47 * 2**20
        ),
    )(device, detail, penalty, angles_t, patch_field, patch_tables, coup)
    return pl.pallas_call(
        add_kernel,
        out_shape=jax.ShapeDtypeStruct(patch_field.shape, F32),
        in_specs=[vspec, vspec],
        out_specs=anyspec,
        scratch_shapes=[big, dma],
        compiler_params=pltpu.CompilerParams(vmem_limit_bytes=16 * 2**20),
    )(part, force)


def solution(mesh):
    devs = mesh.shape["chip"] * mesh.shape["cores"]
    return jax.shard_map(
        functools.partial(shards, devs, round(mesh.shape["chip"] ** (1 / 3)), mesh.shape["cores"]),
        mesh=mesh,
        in_specs=(
            P(("chip", "cores"), None, None, None),
            P(("chip", "cores"), None, None, None),
            P(("chip", "cores"), None, None, None),
            P(),
            P(),
            P(("chip", "cores"), None, None),
            P(("chip", "cores"), None),
        ),
        out_specs=P(("chip", "cores"), None, None, None),
        check_vma=False,
    )
```

```python
import functools

import jax
import jax.numpy as jnp
from jax import lax
from jax.experimental import pallas as pl
from jax.experimental.pallas import tpu as pltpu
from jax.sharding import PartitionSpec as P

BF = jnp.bfloat16
F32 = jnp.float32
MESH = pl.DeviceIdType.MESH
WIDTH = 4


def split(x):
    high = x.astype(BF)
    return high, (x - high.astype(F32)).astype(BF)


def dot(a, b):
    return lax.dot_general(a, b, (((1,), (0,)), ((), ())), preferred_element_type=F32)


def dot_t(a, b):
    return lax.dot_general(a, b, (((1,), (1,)), ((), ())), preferred_element_type=F32)


def prep_field(field, ucat, c):
    h, l = split(field[c])
    cols = slice(c * 128, c * 128 + 128)
    ucat[0:128, cols] = h
    ucat[128:256, cols] = l
    ucat[256:384, cols] = h


def prep_left(tables, tcat, t):
    h, l = split(tables[t])
    rows = slice(t * 128, t * 128 + 128)
    tcat[rows, 0:128] = h
    tcat[rows, 128:256] = h
    tcat[rows, 256:384] = l


def prep_right(tables, rcat, s):
    h, l = split(tables[(4, 3, 5)[s]])
    cols = slice(s * 128, s * 128 + 128)
    rcat[0:128, cols] = h
    rcat[128:256, cols] = l


def prep_coupling(coup, p, cb):
    lane = iota((8, coup.shape[3]), 1)
    for t in range(5):
        for c in range(6):
            tile = jnp.concatenate([coup[t, c], jnp.zeros((2, coup.shape[3]), F32)], axis=0)
            value = jnp.sum(jnp.where(lane == p, tile, 0.0), axis=1, keepdims=True)
            row = (t * 6 + c) * 8
            cb[row : row + 8, :] = jnp.broadcast_to(value, (8, 128))


def left_products(tcat, ucat, prod, m):
    cols = slice(m * 256, m * 256 + 256)
    prod[:, cols] = dot(tcat[...], ucat[:, cols])


def right_products(mixed, rcat, out):
    o = dot_t(mixed[:, 0:384], rcat[...])
    o2 = dot_t(mixed[:, 384:768], rcat[0:128, :])
    for c in range(6):
        q = slice(c * 128, c * 128 + 128)
        out[c] = (o[q, 0:128] + o[q, 128:256]) + o2[q]


def kron_constants(select, high_mask, low_mask, diag):
    row, col = iota(select.shape, 0) // 8, iota(select.shape, 1) // 8
    kind, term = row // 6, col // 6
    used = ((kind == 0) & ((term == 0) | (term >= 3))) | ((kind > 0) & (term == kind))
    select[...] = jnp.where(used & (row % 6 == col % 6), 1.0, 0.0).astype(BF)
    row, col = iota(high_mask.shape, 0), iota(high_mask.shape, 1) // 8
    term, d = row // 48, row % 8
    table = jnp.where(term >= 3, term - 2, term)
    part, block = col // 18, col % 18
    match = (table == block // 6) & (d == block % 6)
    high_mask[...] = jnp.where(match & (part < 2), 1.0, 0.0).astype(BF)
    low_mask[...] = jnp.where(match & (part == 2), 1.0, 0.0).astype(BF)
    row, col = iota(diag.shape, 0), iota(diag.shape, 1)
    diag[...] = jnp.where(row % 8 == col % 8, 1.0, 0.0)


def make_kron(cb, select, high_mask, low_mask, diag, kron):
    h, l = split(cb[...])
    parts = []
    for k in range(0, 432, 128):
        n = min(128, 432 - k)
        cols = slice(k, k + n)
        parts.append(h[:, 0:n] * high_mask[:, cols] + l[:, 0:n] * low_mask[:, cols])
    kron[...] = (dot(select[...], jnp.concatenate(parts, axis=1)) * diag[...]).astype(BF)


def stack_products(prod, pk, m):
    t, d = m // 3, 2 * (m % 3)
    for r in range(16):
        rows = slice(t * 128 + 8 * r, t * 128 + 8 * r + 8)
        x = jnp.concatenate(
            [prod[rows, d * 128 : d * 128 + 128], prod[rows, d * 128 + 128 : d * 128 + 256]], axis=0
        )
        h, l = split(x)
        cols = slice(r * 128, r * 128 + 128)
        pk[16 * m : 16 * m + 16, cols] = h
        pk[144 + 16 * m : 160 + 16 * m, cols] = l
        pk[288 + 16 * m : 304 + 16 * m, cols] = h


def stack(prod, pk, m):
    for t in range(3):
        stack_products(prod, pk, 3 * t + m)


def mix(kron, pk, mixed, m, width):
    o = dot(kron[...], pk[:, m * width * 128 : (m + 1) * width * 128])
    for s in range(3):
        for c in range(6):
            rows = slice((s * 6 + c) * 8, (s * 6 + c) * 8 + 8)
            for r in range(0, width, 2):
                x = jnp.concatenate(
                    [o[rows, r * 128 : r * 128 + 128], o[rows, r * 128 + 128 : r * 128 + 256]], axis=0
                )
                h, l = split(x)
                at = c * 128 + (m * width + r) * 8
                mixed[at : at + 16, s * 128 : s * 128 + 128] = h
                mixed[at : at + 16, 384 + s * 128 : 384 + s * 128 + 128] = l


def far_first(side, inner):
    steps = [
        (x, y, z, core)
        for x in range(side)
        for y in range(side)
        for z in range(side)
        for core in range(inner)
        if x + y + z + core
    ]
    mixed = [steps[(i * 45) % len(steps)] for i in range(len(steps))]
    return sorted(mixed, key=lambda s: -sum(min(k, side - k) for k in s[:3]))


def spline(v):
    m = jnp.abs(v)
    far = jnp.maximum(1.5 - m, 0.0)
    return jnp.where(m < 0.5, 0.75 - m * m, 0.5 * far * far)


def iota(shape, axis):
    return lax.broadcasted_iota(jnp.int32, shape, axis)


def main_kernel(
    devs, side, inner, device_hbm, detail_hbm, penalty_hbm, angles_hbm, field_hbm, tables_hbm, coup_hbm, ov, force,
    uv, tv, cv, u0, u1, t0, t1, r0, r1, p0, p1, w0, w1, k0, k1, pk0, pk1, select, high_mask, low_mask, diag, rot, cb0, cb1,
    device, detail, penalty, angles, comb, ccat, acat, picker, picker_t, taker, taker_t, wts, idx, sbuf, rbuf, bbuf, fbuf,
    in_sem, send_sem, recv_sem, self_sem,
):
    n = uv.shape[0]
    me = lax.axis_index(("chip", "cores"))

    chip_me, core_me = me // inner, me % inner
    my_x, my_y = chip_me // (side * side), chip_me // side % side
    my_zs = [lax.rem(chip_me + k, side) for k in range(side)]
    my_ys = [lax.rem(my_y + k, side) * side for k in range(side)]
    my_xs = [lax.rem(my_x + k, side) * side * side for k in range(side)]
    my_cores = [lax.rem(core_me + k, inner) for k in range(inner)]

    def others():
        for x, y, z, core in far_first(side, inner):
            yield my_xs[x] + my_ys[y] + my_zs[z], my_cores[core]

    barrier = pltpu.get_barrier_semaphore()
    greeted = list(others())

    groups = 4
    per = n // groups
    loads_u = [
        pltpu.make_async_copy(
            field_hbm.at[pl.ds(g * per, per)], uv.at[pl.ds(g * per, per)], in_sem.at[g]
        )
        for g in range(groups)
    ]
    loads_t = [
        pltpu.make_async_copy(
            tables_hbm.at[pl.ds(g * per, per)], tv.at[pl.ds(g * per, per)], in_sem.at[groups + g]
        )
        for g in range(groups)
    ]
    small = [
        pltpu.make_async_copy(src, dst, in_sem.at[2 * groups + i])
        for i, (src, dst) in enumerate(
            ((device_hbm, device), (detail_hbm, detail), (penalty_hbm, penalty), (angles_hbm, angles), (coup_hbm, cv))
        )
    ]
    for copy in small[0:2] + loads_u + small[2:] + loads_t:
        copy.start()

    for who in greeted:
        pl.semaphore_signal(barrier, inc=1, device_id=who, device_id_type=MESH)

    small[0].wait()
    small[1].wait()
    lane = iota((128, 128), 1)
    sub = iota((128, 128), 0)
    lane_f = lane.astype(F32)
    sub_f = sub.astype(F32)
    eye = lane == sub
    hit = device[...] == me
    rid = (detail[:, 1, :] * n + detail[:, 0, :]).astype(F32)
    first = jnp.min(jnp.where(hit, lane_f, 1e6), axis=1, keepdims=True)
    last = jnp.max(jnp.where(hit, lane_f, -1.0), axis=1, keepdims=True)
    row0 = jnp.sum(jnp.where(lane_f == first, rid, 0.0), axis=1, keepdims=True)
    row1 = jnp.sum(jnp.where(lane_f == last, rid, 0.0), axis=1, keepdims=True)
    row0 = jnp.where(last >= 0.0, row0, -1.0)
    row1 = jnp.where(last > first, row1, -1.0)

    def to_row(col):
        return jnp.sum(jnp.where(eye, col, 0.0), axis=0, keepdims=True)

    def one_hot(mask):
        return jnp.where(mask, 1.0, 0.0).astype(BF)

    edge_lane = (lane & 63).astype(F32)
    edge_sub = iota((64, 128), 0).astype(F32)
    for k, row in enumerate((row0, row1)):
        picker[k * 128 : k * 128 + 128, :] = one_hot(row == edge_lane)
        flat = one_hot(to_row(row) == edge_sub)
        picker_t[:, k * 256 : k * 256 + 128] = flat
        picker_t[:, k * 256 + 128 : k * 256 + 256] = flat

    dev_row = device[pl.ds(me, 1), :].astype(F32)
    ln_row = detail[me, 3:4, :].astype(F32)
    st_row = detail[me, 2:3, :].astype(F32)
    order = jnp.where(sub < 64, 2 * sub, 2 * sub - 127)
    perm = lane == order

    def to_col(row):
        return jnp.sum(jnp.where(perm, row, 0.0), axis=1, keepdims=True)

    dev_col, ln, st = to_col(dev_row), to_col(ln_row), to_col(st_row)
    slot = jnp.sum(
        jnp.where((dev_row == dev_col) & (lane < order), 1.0, 0.0), axis=1, keepdims=True
    )
    dev_flat, slot_flat = to_row(dev_col), to_row(slot)
    for k in range(2):
        t = one_hot((lane_f == dev_col) & (slot == float(k)))
        taker[:, k * 256 : k * 256 + 128] = t
        taker[:, k * 256 + 128 : k * 256 + 256] = t
        t = one_hot((sub_f == dev_flat) & (slot_flat == float(k)))
        taker_t[k * 128 : k * 128 + 128, 0:128] = t
        taker_t[k * 128 : k * 128 + 128, 128:256] = t

    def strips(p, carry):
        cols = None
        for c in range(6):
            x = uv[p, c]
            comb[p, c : c + 1, :] = 1.5 * x[0:1] - 0.5 * x[1:2]
            comb[n + p, c : c + 1, :] = 1.5 * x[127:128] - 0.5 * x[126:127]
            x = pltpu.roll(x, 2 + 4 * c, 1)
            cols = x if cols is None else jnp.where(lane < 4 * c, cols, x)
        y = jnp.transpose(cols[:, 0:24])
        for c in range(6):
            y0, y1, y2, y3 = (y[4 * c + k : 4 * c + k + 1] for k in range(4))
            comb[2 * n + p, c : c + 1, :] = 1.5 * y2 - 0.5 * y3
            comb[3 * n + p, c : c + 1, :] = 1.5 * y1 - 0.5 * y0
        return carry

    def strips_pair(i, carry):
        return strips(2 * i + 1, strips(2 * i, carry))

    for g in range(groups):
        loads_u[g].wait()
        lax.fori_loop(g * per // 2, (g + 1) * per // 2, strips_pair, 0)
    for c in range(6):
        h, l = split(comb[:, c, :])
        ccat[0:64, c * 128 : c * 128 + 128] = h
        ccat[64:128, c * 128 : c * 128 + 128] = l
    for k in range(2):
        slots = dot(picker[k * 128 : k * 128 + 128, :], ccat[...])
        for c in range(6):
            sbuf[k * 6 + c] = slots[:, c * 128 : c * 128 + 128]
    pl.semaphore_wait(barrier, devs - 1)

    def exchange(src, dst, which):
        def send(who):
            pltpu.make_async_remote_copy(
                src_ref=src.at[:, who[0] * inner + who[1], :],
                dst_ref=dst.at[:, me, :],
                send_sem=send_sem.at[which],
                recv_sem=recv_sem.at[which],
                device_id=who,
                device_id_type=MESH,
            ).start()

        for who in others():
            send(who)
        pltpu.make_async_copy(src.at[:, me, :], dst.at[:, me, :], self_sem.at[which]).start()

    def settle(src, dst, which):
        others = pl.ds(0, devs - 1)
        for sem in (send_sem, recv_sem):
            pltpu.make_async_copy(src.at[:, others, :], dst.at[:, others, :], sem.at[which]).wait()
        pltpu.make_async_copy(src.at[:, me, :], dst.at[:, me, :], self_sem.at[which]).wait()

    exchange(sbuf, rbuf, 0)

    unit = st * 256.0 + (2.0 * lane_f + 1.0) * ln
    near = jnp.floor((unit + 128.0) * (1.0 / 256.0))
    for tap in range(3):
        j = near + float(tap - 1)
        w = spline(unit * (1.0 / 256.0) - j)
        wts[tap] = jnp.where((j >= 0.0) & (j <= 127.0), w, 0.0)
        idx[tap] = jnp.clip(j, 0.0, 127.0).astype(jnp.int32)
    low = jnp.floor(((256.0 * (lane_f - st) - 384.0) / ln - 1.0) * 0.5) + 1.0
    for tap in range(6):
        q = low + float(tap)
        v = (st * 256.0 + (2.0 * q + 1.0) * ln) * (1.0 / 256.0) - lane_f
        wts[3 + tap] = jnp.where((q >= 0.0) & (q <= 127.0), spline(v), 0.0)
        idx[3 + tap] = jnp.clip(q, 0.0, 127.0).astype(jnp.int32)

    consts = (select, high_mask, low_mask, diag)
    kron_constants(*consts)
    small[3].wait()
    own = n * 4
    half_eye = iota((own, own), 0) == iota((own, own), 1)
    ang = jnp.concatenate(
        [
            jnp.sum(jnp.where(half_eye, angles[k : k + 1, :], 0.0), axis=1, keepdims=True)
            for k in range(3)
        ],
        axis=1,
    )
    cosv, sinv = jnp.cos(ang), jnp.sin(ang)
    ca, cb_, cg = (cosv[:, k : k + 1] for k in range(3))
    sa, sb, sg = (sinv[:, k : k + 1] for k in range(3))
    entries = (
        (cg * cb_, cg * sb * sa - sg * ca, cg * sb * ca + sg * sa),
        (sg * cb_, sg * sb * sa + cg * ca, sg * sb * ca - cg * sa),
        (-sb, cb_ * sa, cb_ * ca),
    )
    for k in range(9):
        rot[k] = jnp.broadcast_to(entries[k // 3][k % 3], (own, 128))

    bufs = ((u0, t0, r0, p0, w0, k0, pk0, cb0), (u1, t1, r1, p1, w1, k1, pk1, cb1))
    small[4].wait()
    prep_coupling(cv, 0, cb0)
    prep_coupling(cv, 1, cb1)
    for copy in loads_t:
        copy.wait()

    def stage(p, j):
        u, t, r, pr, w, kr, pk, cb = bufs[j]
        un, tn, rn, prn, wn, krn, pkn, cbn = bufs[1 - j]
        before = jnp.maximum(p - 1, 0)
        later = jnp.minimum(p + 2, n - 1)
        seqs = (
            [
                lambda: left_products(tn, un, prn, 0),
                lambda: left_products(tn, un, prn, 1),
                lambda: stack(prn, pkn, 0),
                lambda: left_products(tn, un, prn, 2),
                lambda: stack(prn, pkn, 1),
            ]
            + [lambda: mix(kr, pk, w, 0, WIDTH), lambda: stack(prn, pkn, 2)]
            + [lambda k=k: mix(kr, pk, w, k, WIDTH) for k in range(1, 16 // WIDTH)]
            + [
                lambda: right_products(wn, rn, ov.at[before]),
                lambda: make_kron(cbn, *consts, krn),
            ],
            [lambda: prep_coupling(cv, later, cb)]
            + [lambda c=c: prep_field(uv.at[later], u, c) for c in range(6)]
            + [lambda k=k: prep_left(tv.at[later], t, k) for k in range(3)]
            + [lambda k=k: prep_right(tv.at[p], r, k) for k in range(3)],
        )
        keyed = [((i + 0.5) / len(q), f) for q in seqs for i, f in enumerate(q)]
        for _, f in sorted(keyed, key=lambda z: z[0]):
            f()

    def pair(h, carry):
        stage(2 * h, 0)
        stage(2 * h + 1, 1)
        return carry

    for i in range(2):
        for c in range(6):
            prep_field(uv.at[i], bufs[i][0], c)
        for k in range(3):
            prep_left(tv.at[i], bufs[i][1], k)
    for m in range(3):
        left_products(t0, u0, p0, m)
        stack(p0, pk0, m)
    make_kron(cb0, *consts, k0)
    half = n // 4 - 1
    lax.fori_loop(0, half, pair, 0)
    stage(2 * half, 0)

    settle(sbuf, rbuf, 0)

    def slots_of(buf):
        for k in range(2):
            for c in range(6):
                h, l = split(buf[k * 6 + c])
                cols = slice(c * 128, c * 128 + 128)
                acat[k * 256 : k * 256 + 128, cols] = h
                acat[k * 256 + 128 : k * 256 + 256, cols] = l

    slots_of(rbuf)
    strip = dot(taker[...], acat[...])

    def taps(xs, start, count, row):
        totals = [None] * 6
        rows = slice(row, row + 8)
        for tap in range(start, start + count):
            where, weight = idx[tap, rows, :], wts[tap, rows, :]
            for c in range(6):
                v = jnp.take_along_axis(xs[c], where, axis=1) * weight
                totals[c] = v if totals[c] is None else totals[c] + v
        return totals

    def turn(row, entries, values):
        parts = [rot[e, row : row + 8, :] * v for e, v in zip(entries, values)]
        return parts[0] + parts[1] + parts[2]

    small[2].wait()
    for at in range(0, own, 16):
        halves = []
        for row in (at, at + 8):
            near_t, far_t = (
                taps([strip[r : r + 8, c * 128 : c * 128 + 128] for c in range(6)], 0, 3, r)
                for r in (row, own + row)
            )
            near_l, far_l = [], []
            for blk in (0, 3):
                weight = penalty[row : row + 8, blk // 3, :]
                for c in range(3):
                    turned = turn(row, (3 * c, 3 * c + 1, 3 * c + 2), far_t[blk : blk + 3])
                    near_l.append(weight * (near_t[blk + c] - turned))
                for c in range(3):
                    far_l.append(-turn(row, (c, 3 + c, 6 + c), near_l[blk : blk + 3]))
            halves.append((taps(near_l, 3, 6, row), taps(far_l, 3, 6, own + row)))
        for which in range(2):
            base = which * own + at
            for c in range(6):
                h, l = split(jnp.concatenate([halves[0][which][c], halves[1][which][c]], axis=0))
                cols = slice(c * 128, c * 128 + 128)
                acat[base : base + 16, cols] = h
                acat[128 + base : 144 + base, cols] = l
    for k in range(2):
        slots = dot(taker_t[k * 128 : k * 128 + 128, :], acat[0:256, :])
        for c in range(6):
            bbuf[k * 6 + c] = slots[:, c * 128 : c * 128 + 128]
    exchange(bbuf, fbuf, 1)

    stage(2 * half + 1, 1)
    lax.fori_loop(half + 1, n // 2, pair, 0)
    right_products(w1, r1, ov.at[n - 1])

    settle(bbuf, fbuf, 1)
    slots_of(fbuf)
    gathered = dot(picker_t[...], acat[...])
    for c in range(6):
        force[:, c, :] = gathered[:, c * 128 : c * 128 + 128]


def add_kernel(part, force, out_hbm, buf, out_sem):
    n = buf.shape[0]

    def put(p):
        return pltpu.make_async_copy(buf.at[p], out_hbm.at[p], out_sem)

    lane = iota((8, 128), 1)
    sub = iota((8, 128), 0)
    left = jnp.where(lane == 0, 1.5, jnp.where(lane == 1, -0.5, 0.0))
    right = jnp.where(lane == 127, 1.5, jnp.where(lane == 126, -0.5, 0.0))
    spread = jnp.where(sub < 2, left, jnp.where(sub < 4, right, 0.0)).astype(BF)
    top = jnp.where(sub == 0, 1.5, jnp.where(sub == 1, -0.5, 0.0))
    bottom = jnp.where(sub == 7, 1.5, jnp.where(sub == 6, -0.5, 0.0))

    def one(p, carry):
        for c in range(6):
            f0 = force[p, c : c + 1, :]
            f1 = force[n + p, c : c + 1, :]
            f2 = force[2 * n + p, c : c + 1, :]
            f3 = force[3 * n + p, c : c + 1, :]
            h2, l2 = f2.astype(BF).astype(F32), f2 - f2.astype(BF).astype(F32)
            h3, l3 = f3.astype(BF).astype(F32), f3 - f3.astype(BF).astype(F32)
            rows = jnp.where(
                sub == 0, h2, jnp.where(sub == 1, l2, jnp.where(sub == 2, h3, jnp.where(sub == 3, l3, 0.0)))
            ).astype(BF)
            cells = lax.dot_general(
                rows, spread, (((0,), (0,)), ((), ())), preferred_element_type=F32
            )
            buf[p, c] = part[p, c] + cells
            buf[p, c, 0:8, :] = buf[p, c, 0:8, :] + top * f0
            buf[p, c, 120:128, :] = buf[p, c, 120:128, :] + bottom * f1
        put(p).start()
        return carry

    lax.fori_loop(0, n // 2, lambda i, carry: one(2 * i + 1, one(2 * i, carry)), 0)
    pltpu.make_async_copy(buf, out_hbm, out_sem).wait()


def shards(devs, side, inner, patch_field, patch_tables, coupling, side_device, side_detail, penalty, angles):
    n = patch_field.shape[0]
    detail = side_detail.reshape(devs, 128, 4).transpose(0, 2, 1)
    device = side_device.reshape(devs, 128)
    coup = coupling.transpose(1, 2, 3, 0)
    pin = functools.partial(pltpu.with_memory_space_constraint, memory_space=pltpu.HBM)
    device, detail, coup, penalty, angles_t = pin(device), pin(detail), pin(coup), pin(penalty), pin(angles.T)
    anyspec = pl.BlockSpec(memory_space=pltpu.HBM)
    vspec = pl.BlockSpec(memory_space=pltpu.VMEM)
    v = pltpu.VMEM
    big = v(patch_field.shape, F32)
    wire = v((12, devs, 128), F32)
    dma = pltpu.SemaphoreType.DMA
    part, force = pl.pallas_call(
        functools.partial(main_kernel, devs, side, inner),
        out_shape=(
            jax.ShapeDtypeStruct(patch_field.shape, F32),
            jax.ShapeDtypeStruct((4 * n, 6, 128), F32),
        ),
        in_specs=[anyspec] * 7,
        out_specs=(vspec, vspec),
        scratch_shapes=[big, big, v(coup.shape, F32)]
        + [v((384, 768), BF)] * 2
        + [v((384, 384), BF)] * 2
        + [v((256, 384), BF)] * 2
        + [v((384, 768), F32)] * 2
        + [v((768, 768), BF)] * 2
        + [v((144, 432), BF)] * 2
        + [
            v((432, 2048), BF),
            v((432, 2048), BF),
            v((144, 240), BF),
            v((240, 432), BF),
            v((240, 432), BF),
            v((144, 432), F32),
            v((9, penalty.shape[0], 128), F32),
            v((240, 128), F32),
            v((240, 128), F32),
            v((devs, 128), jnp.int32),
            v((devs, 4, 128), jnp.int32),
            v(penalty.shape, F32),
            v((3, penalty.shape[0]), F32),
            v((64, 6, 128), F32),
            v((128, 768), BF),
            v((512, 768), BF),
            v((256, 128), BF),
            v((64, 512), BF),
            v((128, 512), BF),
            v((256, 256), BF),
            v((9, 128, 128), F32),
            v((9, 128, 128), jnp.int32),
        ]
        + [wire] * 4
        + [dma((13,)), dma((2,)), dma((2,)), dma((2,))],
        compiler_params=pltpu.CompilerParams(
            collective_id=0, has_side_effects=True, vmem_limit_bytes=47 * 2**20
        ),
    )(device, detail, penalty, angles_t, patch_field, patch_tables, coup)
    return pl.pallas_call(
        add_kernel,
        out_shape=jax.ShapeDtypeStruct(patch_field.shape, F32),
        in_specs=[vspec, vspec],
        out_specs=anyspec,
        scratch_shapes=[big, dma],
        compiler_params=pltpu.CompilerParams(vmem_limit_bytes=16 * 2**20),
    )(part, force)


def solution(mesh):
    devs = mesh.shape["chip"] * mesh.shape["cores"]
    return jax.shard_map(
        functools.partial(shards, devs, round(mesh.shape["chip"] ** (1 / 3)), mesh.shape["cores"]),
        mesh=mesh,
        in_specs=(
            P(("chip", "cores"), None, None, None),
            P(("chip", "cores"), None, None, None),
            P(("chip", "cores"), None, None, None),
            P(),
            P(),
            P(("chip", "cores"), None, None),
            P(("chip", "cores"), None),
        ),
        out_specs=P(("chip", "cores"), None, None, None),
        check_vma=False,
    )
```
